32 devices in a mesh: seq: 8 (over z, y), head: 4 (over x, core).
Axes of the slice: x: 2, y: 2, z: 4, core: 2. Of those that a mesh axis runs over, the one named last changes fastest.
Arguments:
- tokens: bfloat16 [1024, 2048], P('seq'), may hold values from -20 to 20, as said below
- projection: bfloat16 [2048, 3072], P(None, 'head'), may hold values from -0.078125 to 0.078125
- context_cotangent: bfloat16 [1024, 2048], P('seq', 'head'), may hold values from -80 to 80
Outputs:
- perturbed_context: bfloat16 [1024, 2048], P('seq', 'head')
- ascent_direction: float32 [2048, 3072], P('seq', 'head')
The draws below stay inside these ranges and needn't reach their ends.
Inputs may be any that keep to these rules, and one draw needn't show every extreme that they name: `tokens`: activations of the layer.
All inputs are finite; a program needn't handle non-finite values.
Results may differ from the reference program's by a relative error of at most 0.017.
Values may be sent and summed in bfloat16 or wider, within the bound.
A program may use at most 64 MiB of HBM per device.

```python
import math
import jax
import jax.numpy as jnp
from jax import lax

INPUT_FEATURES = 2048
HQ = 16
KEY_VALUE_HEADS = 4
HEAD_DIMENSION = 128
QUERY_PER_GROUP = 4
CW = 3072
SEQUENCE_TOKENS = 1024


def draw_tokens(key, part):
    key_list = jax.random.split(key, 2)
    ramp = 0.7 * 10.0 ** (jnp.arange(INPUT_FEATURES, dtype=jnp.float32) / max(INPUT_FEATURES - 1, 1) - 0.5)
    jitter = jax.random.uniform(key_list[1], (INPUT_FEATURES,), jnp.float32, 0.7, 1.4)
    base = jnp.clip(jax.random.normal(key_list[0], (SEQUENCE_TOKENS, INPUT_FEATURES), jnp.float32), -6.0, 6.0)
    return (base * ramp * jitter).astype(jnp.bfloat16)


def draw_context_cotangent(key, part):
    key_list = jax.random.split(key, 2)
    head_index = (jnp.arange(HQ * HEAD_DIMENSION, dtype=jnp.int32) // HEAD_DIMENSION).astype(jnp.float32)
    head_scale = 0.3 * 10.0 ** (head_index / max(HQ - 1, 1))
    rough = jax.random.uniform(key_list[1], (SEQUENCE_TOKENS, 1), jnp.float32, 0.5, 1.5)
    base = jnp.clip(jax.random.normal(key_list[0], (SEQUENCE_TOKENS, HQ * HEAD_DIMENSION), jnp.float32), -6.0, 6.0)
    return (base * rough * head_scale).astype(jnp.bfloat16)


def levels(key, dims, cuts, low, top_value):
    def one(position, blocks):
        heights = jax.random.uniform(jax.random.fold_in(jax.random.fold_in(key, 6), position), (blocks,), jnp.float32, low / len(cuts), top_value / len(cuts))
        return jnp.repeat(jnp.exp(heights), dims[position] // blocks).reshape((-1,) + (1,) * (len(dims) - position - 1))

    level = one(*cuts[0])
    for cut in cuts[1:]:
        level = level * one(*cut)
    return level


def noise(stream_key, dims, scale, bound, pieces=(), held_as=jnp.bfloat16):
    entries = jax.random.normal(stream_key, dims, jnp.float32) * scale
    if len(pieces) > 0:
        entries = levels(stream_key, dims, pieces, -0.22, 0.18) * entries
    return jnp.clip(entries, min=-bound, max=bound).astype(held_as)


def setup_inputs(seed: int = 0) -> dict:
    key_of = jax.random.split(jax.random.key(seed), 4)
    return {
        "tokens": draw_tokens(jax.random.fold_in(key_of[3], 71), 0),
        "projection": noise(key_of[1], (INPUT_FEATURES, CW), (INPUT_FEATURES * 3) ** -0.5, 0.078125, ((1, 4),)),
        "context_cotangent": draw_context_cotangent(jax.random.fold_in(key_of[3], 71), 0),
    }


masked_score = -1e+30

def rounded(values):
    return lax.optimization_barrier(values.astype(jnp.bfloat16)).astype(jnp.float32)

def split_heads(projected_weight):
    reshaped_grads = projected_weight.reshape(projected_weight.shape[0], KEY_VALUE_HEADS, QUERY_PER_GROUP + 2, HEAD_DIMENSION)
    query = jnp.moveaxis(reshaped_grads[:, :, :QUERY_PER_GROUP], 1, 0)
    key_rows = jnp.moveaxis(reshaped_grads[:, :, QUERY_PER_GROUP], 1, 0)
    value_rows = jnp.moveaxis(reshaped_grads[:, :, QUERY_PER_GROUP + 1], 1, 0)
    return (query, key_rows, value_rows)

def block_scores(query_block, key_rows, positions):
    scores = jnp.einsum('tgd,kd->tgk', query_block.astype(jnp.float32), key_rows.astype(jnp.float32)) * HEAD_DIMENSION ** (-0.5)
    key_pos = jnp.arange(key_rows.shape[0], dtype=jnp.int32)
    allowed = key_pos[None, None, :] <= positions[:, None, None]
    return jnp.where(allowed, scores, masked_score)

def forward_group(query, key_rows, value_rows):
    query_span = min(512, SEQUENCE_TOKENS)
    count_blocks = SEQUENCE_TOKENS // query_span
    blocks = query.reshape(count_blocks, query_span, QUERY_PER_GROUP, HEAD_DIMENSION)

    def per_block(inputs):
        block_index, query_block = inputs
        positions = block_index * query_span + jnp.arange(query_span, dtype=jnp.int32)
        scores = block_scores(query_block, key_rows, positions)
        row_max = lax.optimization_barrier(jnp.max(scores, axis=-1, keepdims=True))
        weights = jnp.exp(scores - row_max)
        row_total = lax.optimization_barrier(jnp.sum(weights, axis=-1, keepdims=True))
        context = jnp.einsum('tgk,kd->tgd', weights, value_rows.astype(jnp.float32), precision=lax.Precision.HIGHEST) / row_total
        return (context.astype(jnp.bfloat16), (row_max + jnp.log(row_total))[..., 0])
    context, log_total = lax.map(per_block, (jnp.arange(count_blocks, dtype=jnp.int32), blocks))
    return (context.reshape(SEQUENCE_TOKENS, QUERY_PER_GROUP, HEAD_DIMENSION), log_total.reshape(SEQUENCE_TOKENS, QUERY_PER_GROUP))

def backward_group(query, key_rows, value_rows, context, log_total, grad_out):
    query_span = min(512, SEQUENCE_TOKENS)
    count_blocks = SEQUENCE_TOKENS // query_span
    score_scale = HEAD_DIMENSION ** (-0.5)
    row_delta = lax.optimization_barrier(jnp.sum(grad_out.astype(jnp.float32) * context.astype(jnp.float32), axis=-1))
    keys_f = key_rows.astype(jnp.float32)
    values_f = value_rows.astype(jnp.float32)

    def per_block(carry, inputs):
        key_grad, value_grad = carry
        block_index, query_block, grad_block, lse_block, delta_block = inputs
        positions = block_index * query_span + jnp.arange(query_span, dtype=jnp.int32)
        scores = block_scores(query_block, key_rows, positions)
        probs_full = jnp.exp(scores - lse_block[..., None])
        grad_f = grad_block.astype(jnp.float32)
        prob_grad = jnp.einsum('tgd,kd->tgk', grad_f, values_f)
        score_grad = rounded(probs_full * (prob_grad - delta_block[..., None]) * score_scale)
        query_grad = jnp.einsum('tgk,kd->tgd', score_grad, keys_f).astype(jnp.bfloat16)
        key_grad = key_grad + jnp.einsum('tgk,tgd->kd', score_grad, query_block.astype(jnp.float32))
        value_grad = value_grad + jnp.einsum('tgk,tgd->kd', rounded(probs_full), grad_f)
        return ((key_grad, value_grad), query_grad)
    initial = (jnp.zeros((SEQUENCE_TOKENS, HEAD_DIMENSION), jnp.float32), jnp.zeros((SEQUENCE_TOKENS, HEAD_DIMENSION), jnp.float32))
    inputs = (jnp.arange(count_blocks, dtype=jnp.int32), query.reshape(count_blocks, query_span, QUERY_PER_GROUP, HEAD_DIMENSION), grad_out.reshape(count_blocks, query_span, QUERY_PER_GROUP, HEAD_DIMENSION), log_total.reshape(count_blocks, query_span, QUERY_PER_GROUP), row_delta.reshape(count_blocks, query_span, QUERY_PER_GROUP))
    (key_grad, value_grad), query_grad = lax.scan(per_block, initial, inputs)
    return (query_grad.reshape(SEQUENCE_TOKENS, QUERY_PER_GROUP, HEAD_DIMENSION), key_grad.astype(jnp.bfloat16), value_grad.astype(jnp.bfloat16))

def reference(tokens, projection, context_cotangent):
    projected_weight = jnp.dot(tokens, projection, preferred_element_type=jnp.float32).astype(jnp.bfloat16)
    query, key_rows, value_rows = split_heads(projected_weight)
    gradient_by_group = jnp.moveaxis(context_cotangent.reshape(SEQUENCE_TOKENS, KEY_VALUE_HEADS, QUERY_PER_GROUP, HEAD_DIMENSION), 1, 0)

    def group_pass(inputs):
        query_one, key_one, value_one, grad_one = inputs
        context, log_total = forward_group(query_one, key_one, value_one)
        return backward_group(query_one, key_one, value_one, context, log_total, grad_one)
    query_grad, key_grad, value_grad = lax.map(group_pass, (query, key_rows, value_rows, gradient_by_group))
    head_grads = jnp.concatenate([jnp.moveaxis(query_grad, 0, 1), jnp.moveaxis(key_grad, 0, 1)[:, :, None, :], jnp.moveaxis(value_grad, 0, 1)[:, :, None, :]], axis=2).reshape(SEQUENCE_TOKENS, CW)
    weight_grad = jnp.dot(tokens.T, head_grads, preferred_element_type=jnp.float32)
    grad_norm = jnp.sqrt(jnp.sum(weight_grad * weight_grad))
    direction = weight_grad * (math.sqrt(INPUT_FEATURES * CW) / grad_norm)
    moved_weights = (projection.astype(jnp.float32) + 0.2 * math.sqrt(CW) / grad_norm * weight_grad).astype(jnp.bfloat16)
    projected_new = jnp.dot(tokens, moved_weights, preferred_element_type=jnp.float32).astype(jnp.bfloat16)
    query_new, key_new, value_new = split_heads(projected_new)

    def forward_only(inputs):
        return forward_group(inputs[0], inputs[1], inputs[2])[0]
    context_new = lax.map(forward_only, (query_new, key_new, value_new))
    perturbed = jnp.moveaxis(context_new, 0, 1).reshape(SEQUENCE_TOKENS, HQ * HEAD_DIMENSION)
    return (perturbed, direction)
```

```python
import functools
import math

import jax
import jax.numpy as jnp
from jax import lax
from jax.experimental import pallas as pl
from jax.experimental.pallas import tpu as pltpu
from jax.sharding import PartitionSpec as P

INPUT_FEATURES = 2048
KEY_VALUE_HEADS = 4
HEAD_DIMENSION = 128
QUERY_PER_GROUP = 4


masked_score = -1e30
key_block = 512


def attend_fold(query_rows, query_pos, score_scale):
    head_size = query_rows.shape[1]

    def single_block(carry_state, block_rows, offset):
        running_max, row_total, context_sum = carry_state
        key_rows = block_rows[:, :head_size]
        value_rows = block_rows[:, head_size:].astype(jnp.float32)
        scores = jnp.dot(query_rows, key_rows.T, preferred_element_type=jnp.float32) * score_scale
        key_pos = offset + jnp.arange(block_rows.shape[0], dtype=jnp.int32)
        allowed = key_pos[None, :] <= query_pos[:, None]
        scores = jnp.where(allowed, scores, masked_score)
        new_max = jnp.maximum(running_max, jnp.max(scores, axis=1))
        factor = jnp.exp(running_max - new_max)
        weights = jnp.where(allowed, jnp.exp(scores - new_max[:, None]), 0.0)
        row_total = row_total * factor + jnp.sum(weights, axis=1)
        context_sum = context_sum * factor[:, None] + jnp.dot(
            weights, value_rows, precision=lax.Precision.HIGHEST, preferred_element_type=jnp.float32
        )
        return (new_max, row_total, context_sum)

    def fold_keys(carry_state, block_rows, offset):
        row_count = block_rows.shape[0]
        if row_count > key_block and row_count % key_block == 0:

            def sub_block(block_index, inner_state):
                part_rows = lax.dynamic_slice_in_dim(
                    block_rows, block_index * key_block, key_block, 0
                )
                return single_block(inner_state, part_rows, block_index * key_block)

            return lax.fori_loop(0, row_count // key_block, sub_block, carry_state)
        return single_block(carry_state, block_rows, offset)

    return fold_keys


def on_device(tokens, projection, context_cotangent):
    score_scale = HEAD_DIMENSION ** (-0.5)
    local_rows = tokens.shape[0]
    rows_all = local_rows * QUERY_PER_GROUP
    first_row = lax.axis_index("seq") * local_rows
    query_pos = first_row + jnp.arange(rows_all, dtype=jnp.int32) // QUERY_PER_GROUP

    def split_heads(projected_weight):
        reshaped_grads = projected_weight.reshape(local_rows, QUERY_PER_GROUP + 2, HEAD_DIMENSION)
        query_rows = reshaped_grads[:, :QUERY_PER_GROUP].reshape(rows_all, HEAD_DIMENSION)
        key_value = reshaped_grads[:, QUERY_PER_GROUP:].reshape(local_rows, 2 * HEAD_DIMENSION)
        return (query_rows, key_value)

    def empty_state():
        return (
            jnp.full((rows_all,), masked_score, jnp.float32),
            jnp.zeros((rows_all,), jnp.float32),
            jnp.zeros((rows_all, HEAD_DIMENSION), jnp.float32),
        )

    projected_weight = jnp.dot(tokens, projection, preferred_element_type=jnp.float32).astype(
        jnp.bfloat16
    )
    query_rows, key_value = split_heads(projected_weight)
    gathered = lax.all_gather(key_value, "seq", axis=0, tiled=True)
    total_rows = gathered.shape[0]
    block_size = min(key_block, total_rows)
    needed = (first_row + local_rows - 1) // block_size + 1
    fold_first = attend_fold(query_rows, query_pos, score_scale)

    def forward_step(block_index, carry_state):
        block_rows = lax.dynamic_slice_in_dim(gathered, block_index * block_size, block_size, 0)
        return fold_first(carry_state, block_rows, block_index * block_size)

    running_max, row_total, context_sum = lax.fori_loop(0, needed, forward_step, empty_state())
    context = (context_sum / row_total[:, None]).astype(jnp.bfloat16)
    log_total = running_max + jnp.log(row_total)
    grad_rows = context_cotangent.reshape(rows_all, HEAD_DIMENSION)
    row_delta = jnp.sum(grad_rows.astype(jnp.float32) * context.astype(jnp.float32), axis=1)
    contract_rows = (((0,), (0,)), ((), ()))

    def backward_step(block_index, carry_state):
        query_grad, key_terms = carry_state
        offset = block_index * block_size
        block_rows = lax.dynamic_slice_in_dim(gathered, offset, block_size, 0)
        key_rows = block_rows[:, :HEAD_DIMENSION]
        value_rows = block_rows[:, HEAD_DIMENSION:]
        scores = jnp.dot(query_rows, key_rows.T, preferred_element_type=jnp.float32) * score_scale
        key_pos = offset + jnp.arange(block_size, dtype=jnp.int32)
        allowed = key_pos[None, :] <= query_pos[:, None]
        probs_full = jnp.where(allowed, jnp.exp(scores - log_total[:, None]), 0.0)
        probs_half = probs_full.astype(jnp.bfloat16)
        prob_grad = jnp.dot(grad_rows, value_rows.T, preferred_element_type=jnp.float32)
        score_grad = (probs_full * (prob_grad - row_delta[:, None]) * score_scale).astype(
            jnp.bfloat16
        )
        query_grad = query_grad + jnp.dot(score_grad, key_rows, preferred_element_type=jnp.float32)
        key_grad = lax.dot_general(
            score_grad, query_rows, contract_rows, preferred_element_type=jnp.float32
        )
        value_grad = lax.dot_general(
            probs_half, grad_rows, contract_rows, preferred_element_type=jnp.float32
        )
        key_terms = lax.dynamic_update_slice_in_dim(
            key_terms, jnp.concatenate([key_grad, value_grad], axis=1), offset, 0
        )
        return (query_grad, key_terms)

    initial = (
        jnp.zeros((rows_all, HEAD_DIMENSION), jnp.float32),
        jnp.zeros((total_rows, 2 * HEAD_DIMENSION), jnp.float32),
    )
    query_grad, key_terms = lax.fori_loop(0, needed, backward_step, initial)
    key_value_grad = lax.psum_scatter(key_terms, "seq", scatter_dimension=0, tiled=True).astype(
        jnp.bfloat16
    )
    head_grads = jnp.concatenate(
        [
            query_grad.astype(jnp.bfloat16).reshape(local_rows, QUERY_PER_GROUP * HEAD_DIMENSION),
            key_value_grad,
        ],
        axis=1,
    )
    grad_term = lax.dot_general(
        tokens, head_grads, contract_rows, preferred_element_type=jnp.float32
    )
    normalizing_scale = math.sqrt(
        INPUT_FEATURES * KEY_VALUE_HEADS * (QUERY_PER_GROUP + 2) * HEAD_DIMENSION
    )
    ascent_radius = 0.2 * math.sqrt(KEY_VALUE_HEADS * (QUERY_PER_GROUP + 2) * HEAD_DIMENSION)
    weight_grad = lax.psum(grad_term, "seq")
    square_sum = lax.psum(jnp.sum(weight_grad * weight_grad), "head")
    grad_norm = jnp.sqrt(square_sum)
    share_rows = INPUT_FEATURES // lax.axis_size("seq")
    own_grad = lax.dynamic_slice_in_dim(
        weight_grad, lax.axis_index("seq") * share_rows, share_rows, 0
    )
    direction = own_grad * (normalizing_scale / grad_norm)
    moved_weights = (
        projection.astype(jnp.float32) + ascent_radius / grad_norm * weight_grad
    ).astype(jnp.bfloat16)
    projected_new = jnp.dot(tokens, moved_weights, preferred_element_type=jnp.float32).astype(
        jnp.bfloat16
    )
    query_new, key_value_new = split_heads(projected_new)
    fold_new = attend_fold(query_new, query_pos, score_scale)
    final_state = fold_new(
        empty_state(), lax.all_gather(key_value_new, "seq", axis=0, tiled=True), jnp.int32(0)
    )
    perturbed = (
        (final_state[2] / final_state[1][:, None])
        .astype(jnp.bfloat16)
        .reshape(local_rows, QUERY_PER_GROUP * HEAD_DIMENSION)
    )
    return (perturbed, direction)


def exchange_kernel(seq_size, tokens_ref, cotangent_ref, tokens_out, cotangent_out, *sems):
    (local_sem, own_sent, own_sent_c, fold_sent, fold_sent_c, got, got_c,
     across_sent, pair_sent, relay_sent, across_got, pair_got, relay_got) = sems
    s = lax.axis_index("seq")
    h = lax.axis_index("head")
    rows_here = tokens_ref.shape[0]
    parts = tokens_out.shape[0]
    width = tokens_out.shape[2]

    def flip(index, mask):
        bit = 1
        while bit <= mask:
            if mask & bit:
                index = index + bit - 2 * bit * ((index // bit) % 2)
            bit *= 2
        return index

    def rows(index):
        return pl.ds(pl.multiple_of(index * rows_here, rows_here), rows_here)

    def columns(index):
        return pl.ds(pl.multiple_of(index * width, width), width)

    def remote(source, target, send, receive, mask_s, mask_h):
        return pltpu.make_async_remote_copy(
            src_ref=source, dst_ref=target, send_sem=send, recv_sem=receive,
            device_id=(flip(s, mask_s), flip(h, mask_h)), device_id_type=pl.DeviceIdType.MESH,
        )

    even = [k for k in range(2, seq_size, 2)]
    direct = [1] + even
    barrier = pltpu.get_barrier_semaphore()
    greeted = [(k, 0) for k in direct] + [(0, 1), (0, 2)]
    for mask_s, mask_h in greeted:
        pl.semaphore_signal(barrier, inc=1, device_id=(flip(s, mask_s), flip(h, mask_h)),
                            device_id_type=pl.DeviceIdType.MESH)
    pl.semaphore_wait(barrier, len(greeted))

    own_tokens = tokens_ref.at[:, columns(h)]
    own_place = tokens_out.at[h, rows(s)]
    own_place_c = cotangent_out.at[rows(s)]
    sent = []
    for k in even + [1]:
        copy = remote(own_tokens, own_place, own_sent.at[k], got.at[k], k, 0)
        copy.start()
        sent.append(copy)
    for k in even + [1]:
        copy = remote(cotangent_ref, own_place_c, own_sent_c.at[k], got_c.at[k], k, 0)
        copy.start()
        sent.append(copy)
    local = [pltpu.make_async_copy(tokens_ref.at[:, columns(q)], tokens_out.at[q, rows(s)],
                                   local_sem.at[q]) for q in range(parts)]
    local.append(pltpu.make_async_copy(cotangent_ref, own_place_c, local_sem.at[parts]))
    for copy in local:
        copy.start()

    def arrived(k):
        place = tokens_out.at[h, rows(flip(s, k))]
        remote(place, place, own_sent.at[0], got.at[k], 1, 0).wait_recv()
        if k % 2 == 0:
            copy = remote(place, place, fold_sent.at[k], got.at[k + 1], 1, 0)
            copy.start()
            sent.append(copy)
        for semaphores, mask in (((across_sent, across_got), 2), ((pair_sent, pair_got), 1)):
            copy = remote(place, place, semaphores[0].at[k], semaphores[1].at[k], 0, mask)
            copy.start()
            sent.append(copy)

    def arrived_c(k):
        place = cotangent_out.at[rows(flip(s, k))]
        remote(place, place, own_sent.at[0], got_c.at[k], 1, 0).wait_recv()
        if k % 2 == 0:
            copy = remote(place, place, fold_sent_c.at[k], got_c.at[k + 1], 1, 0)
            copy.start()
            sent.append(copy)

    def relay(k):
        place = tokens_out.at[flip(h, 2), rows(flip(s, k))]
        remote(place, place, own_sent.at[0], across_got.at[k], 0, 2).wait_recv()
        copy = remote(place, place, relay_sent.at[k], relay_got.at[k], 0, 1)
        copy.start()
        sent.append(copy)

    order = [even[0], 1] + even[1:] + [k + 1 for k in even]
    for position, k in enumerate(order):
        arrived(k)
        if k % 2 == 0:
            arrived_c(k)
        if position >= 2:
            relay(order[position - 2])
    for k in order[-2:]:
        relay(k)
    for k in order:
        if k % 2:
            arrived_c(k)
    for k in order:
        place = tokens_out.at[flip(h, 1), rows(flip(s, k))]
        remote(place, place, own_sent.at[0], pair_got.at[k], 0, 1).wait_recv()
        place = tokens_out.at[flip(h, 3), rows(flip(s, k))]
        remote(place, place, own_sent.at[0], relay_got.at[k], 0, 1).wait_recv()
    for copy in sent:
        copy.wait_send()
    for copy in local:
        copy.wait()


def exchange(tokens, cotangent, seq_size, parts):
    local_rows, features = tokens.shape
    total = local_rows * seq_size
    return pl.pallas_call(
        functools.partial(exchange_kernel, seq_size),
        out_shape=(
            jax.ShapeDtypeStruct((parts, total, features // parts), tokens.dtype),
            jax.ShapeDtypeStruct((total, cotangent.shape[1]), cotangent.dtype),
        ),
        in_specs=[pl.BlockSpec(memory_space=pltpu.VMEM)] * 2,
        out_specs=(pl.BlockSpec(memory_space=pltpu.VMEM),) * 2,
        scratch_shapes=[pltpu.SemaphoreType.DMA((parts + 1,))]
        + [pltpu.SemaphoreType.DMA((seq_size,))] * 12,
        compiler_params=pltpu.CompilerParams(collective_id=0, has_side_effects=True),
        name="exchange",
    )(tokens, cotangent)


CONTRACT_LAST = (((1,), (1,)), ((), ()))
CONTRACT_FIRST = (((0,), (0,)), ((), ()))
SCALE = HEAD_DIMENSION ** (-0.5)
SCALE_LOG2 = SCALE * math.log2(math.e)
QW = QUERY_PER_GROUP * HEAD_DIMENSION
D = HEAD_DIMENSION


def gradient_kernel(
    tokens, projection, cotangent, own_grad, squares, base_q, base_kv, move_q, move_kv,
    projected, base, key_t, value_t, grads, key_sum, value_sum, weight_half,
):
    s = lax.axis_index("seq")
    parts, total, width = tokens.shape
    tile = min(256, total)
    local_rows = base_q.shape[0]
    share = own_grad.shape[0]

    def token_rows(rows, weights, columns):
        acc = jnp.dot(tokens[0, rows, :], weights[pl.ds(0, width), columns],
                      preferred_element_type=jnp.float32)
        for q in range(1, parts):
            acc += jnp.dot(tokens[q, rows, :], weights[pl.ds(q * width, width), columns],
                           preferred_element_type=jnp.float32)
        return acc

    @pl.loop(0, total // tile)
    def _(block):
        rows = pl.ds(pl.multiple_of(block * tile, tile), tile)
        acc = token_rows(rows, projection, slice(None))
        base[rows, :] = acc
        half = acc.astype(jnp.bfloat16)
        projected[rows, :] = half
        half_f = half.astype(jnp.float32)
        key_t[:, rows] = half_f[:, QW : QW + D].T.astype(jnp.bfloat16)
        value_t[:, rows] = half_f[:, QW + D :].T.astype(jnp.bfloat16)

    own_rows = pl.ds(pl.multiple_of(s * local_rows, local_rows), local_rows)
    base_q[...] = base[own_rows, :QW]
    base_kv[...] = base[:, QW:]
    key_sum[...] = jnp.zeros_like(key_sum)
    value_sum[...] = jnp.zeros_like(value_sum)

    allowed = lax.broadcasted_iota(jnp.int32, (tile, tile), 0) <= lax.broadcasted_iota(
        jnp.int32, (tile, tile), 1
    )
    for block in range(total // tile):
        length = (block + 1) * tile
        rows = slice(block * tile, length)

        @pl.loop(0, QUERY_PER_GROUP)
        def _(head):
            columns = pl.ds(pl.multiple_of(head * D, D), D)
            query = projected[rows, columns]
            out_grad = cotangent[rows, columns]
            scores = lax.dot_general(projected[:length, QW : QW + D], query, CONTRACT_LAST,
                                     preferred_element_type=jnp.float32)
            last = jnp.where(allowed, scores[block * tile :], masked_score)
            scores = last if block == 0 else jnp.concatenate([scores[: block * tile], last], 0)
            top = jnp.max(scores, axis=0, keepdims=True)
            weights = jnp.exp2(scores * SCALE_LOG2 - top * SCALE_LOG2)
            probs = weights * (1.0 / jnp.sum(weights, axis=0, keepdims=True))
            probs_half = probs.astype(jnp.bfloat16)
            context_t = jnp.dot(value_t[:, :length], probs_half,
                                preferred_element_type=jnp.float32)
            context_t = context_t.astype(jnp.bfloat16).astype(jnp.float32)
            delta = jnp.sum(out_grad.astype(jnp.float32).T * context_t, axis=0, keepdims=True)
            prob_grad = lax.dot_general(projected[:length, QW + D :], out_grad, CONTRACT_LAST,
                                        preferred_element_type=jnp.float32)
            score_grad = (probs * (prob_grad - delta)).astype(jnp.bfloat16)
            query_t = jnp.dot(key_t[:, :length], score_grad, preferred_element_type=jnp.float32)
            grads[rows, columns] = (query_t * SCALE).T.astype(jnp.bfloat16)
            key_sum[:length, :] += jnp.dot(score_grad, query, preferred_element_type=jnp.float32)
            value_sum[:length, :] += jnp.dot(probs_half, out_grad,
                                             preferred_element_type=jnp.float32)

    grads[:, QW : QW + D] = (key_sum[...] * SCALE).astype(jnp.bfloat16)
    grads[:, QW + D :] = value_sum[...].astype(jnp.bfloat16)

    squares[...] = jnp.zeros_like(squares)
    per_part = width // share

    @pl.loop(0, parts * per_part)
    def _(chunk):
        columns = pl.ds(pl.multiple_of((chunk % per_part) * share, share), share)
        rows = pl.ds(pl.multiple_of(chunk * share, share), share)
        block = lax.dot_general(tokens[chunk // per_part, :, columns], grads[...], CONTRACT_FIRST,
                                preferred_element_type=jnp.float32)
        squares[...] += jnp.sum(block * block, axis=0, keepdims=True)
        weight_half[rows, :] = block.astype(jnp.bfloat16)

        @pl.when(chunk == s)
        def _():
            own_grad[...] = block

    move_q[...] = token_rows(own_rows, weight_half, slice(0, QW))

    @pl.loop(0, total // tile)
    def _(block):
        rows = pl.ds(pl.multiple_of(block * tile, tile), tile)
        move_kv[rows, :] = token_rows(rows, weight_half, slice(QW, None))


def gradients(tokens_all, projection, cotangent_all, local_rows, share):
    parts, total, width = tokens_all.shape
    features, columns = projection.shape
    f32, bf16 = jnp.float32, jnp.bfloat16
    shape = jax.ShapeDtypeStruct
    return pl.pallas_call(
        gradient_kernel,
        out_shape=(
            shape((share, columns), f32),
            shape((1, columns), f32),
            shape((local_rows, QW), f32),
            shape((total, 2 * D), f32),
            shape((local_rows, QW), f32),
            shape((total, 2 * D), f32),
        ),
        in_specs=[pl.BlockSpec(memory_space=pltpu.VMEM)] * 3,
        out_specs=(pl.BlockSpec(memory_space=pltpu.VMEM),) * 6,
        scratch_shapes=[
            pltpu.VMEM((total, columns), bf16),
            pltpu.VMEM((total, columns), f32),
            pltpu.VMEM((D, total), bf16),
            pltpu.VMEM((D, total), bf16),
            pltpu.VMEM((total, columns), bf16),
            pltpu.VMEM((total, D), f32),
            pltpu.VMEM((total, D), f32),
            pltpu.VMEM((features, columns), bf16),
        ],
        compiler_params=pltpu.CompilerParams(vmem_limit_bytes=VMEM_BUDGET),
        name="gradients",
    )(tokens_all, projection, cotangent_all)


def perturbed_kernel(radius, root, norm_ref, own_grad, base_q, base_kv, move_q, move_kv, out,
                     direction):
    s = lax.axis_index("seq")
    inverse = 1.0 / norm_ref[...]
    direction[...] = own_grad[...] * (root * inverse)
    step = radius * inverse
    local_rows = base_q.shape[0]
    total = base_kv.shape[0]
    query = (base_q[...] + step * move_q[...]).astype(jnp.bfloat16)
    key_value = (base_kv[...] + step * move_kv[...]).astype(jnp.bfloat16)
    value_t = key_value[:, D:].astype(jnp.float32).T.astype(jnp.bfloat16)
    stacked = jnp.concatenate(
        [query[:, g * D : (g + 1) * D] for g in range(QUERY_PER_GROUP)], axis=0
    )
    scores = lax.dot_general(key_value[:, :D], stacked, CONTRACT_LAST,
                             preferred_element_type=jnp.float32)
    key_pos = lax.broadcasted_iota(jnp.int32, (total, local_rows), 0)
    row_pos = lax.broadcasted_iota(jnp.int32, (total, local_rows), 1) + s * local_rows
    allowed = key_pos <= row_pos
    for g in range(QUERY_PER_GROUP):
        part = jnp.where(allowed, scores[:, g * local_rows : (g + 1) * local_rows], masked_score)
        top = jnp.max(part, axis=0, keepdims=True)
        weights = jnp.exp2(part * SCALE_LOG2 - top * SCALE_LOG2)
        sums = jnp.sum(weights, axis=0, keepdims=True)
        context_t = jnp.dot(value_t, weights.astype(jnp.bfloat16),
                            preferred_element_type=jnp.float32) / sums
        out[:, g * D : (g + 1) * D] = context_t.T.astype(jnp.bfloat16)


VMEM_BUDGET = 60 * 1024 * 1024


def resident_step(tokens, projection, context_cotangent):
    seq_size, head_size = lax.axis_size("seq"), lax.axis_size("head")
    local_rows, features = tokens.shape
    columns = projection.shape[1]
    share = features // seq_size
    tokens_all, cotangent_all = exchange(tokens, context_cotangent, seq_size, head_size)
    own_grad, squares, base_q, base_kv, move_q, move_kv = gradients(
        tokens_all, projection, cotangent_all, local_rows, share
    )
    grad_norm = jnp.sqrt(lax.psum(jnp.sum(squares), "head")).reshape(1, 1)
    root = math.sqrt(features * head_size * columns)
    radius = 0.2 * math.sqrt(head_size * columns)
    return pl.pallas_call(
        functools.partial(perturbed_kernel, radius, root),
        out_shape=(
            jax.ShapeDtypeStruct((local_rows, QW), jnp.bfloat16),
            jax.ShapeDtypeStruct((share, columns), jnp.float32),
        ),
        in_specs=[pl.BlockSpec(memory_space=pltpu.VMEM)] * 6,
        out_specs=(pl.BlockSpec(memory_space=pltpu.VMEM),) * 2,
        compiler_params=pltpu.CompilerParams(vmem_limit_bytes=VMEM_BUDGET),
        name="perturbed",
    )(grad_norm, own_grad, base_q, base_kv, move_q, move_kv)


def fits(local_rows, features, columns, seq_size, head_size):
    total = local_rows * seq_size
    share = features // seq_size
    held = total * (2 * features + 2 * QW + 12 * columns + 24 * D) + 4 * features * columns
    pairs = seq_size >= 4 and seq_size & (seq_size - 1) == 0 and head_size == 4
    aligned = share % 128 == 0 and (features // head_size) % share == 0 and local_rows % 128 == 0
    return pairs and aligned and held < VMEM_BUDGET // 2


def step(tokens, projection, context_cotangent):
    sizes = (*tokens.shape, projection.shape[1], lax.axis_size("seq"), lax.axis_size("head"))
    if fits(*sizes):
        return resident_step(tokens, projection, context_cotangent)
    return on_device(tokens, projection, context_cotangent)


def solution(mesh):
    return jax.shard_map(
        step,
        mesh=mesh,
        in_specs=(P("seq", None), P(None, "head"), P("seq", "head")),
        out_specs=(P("seq", "head"), P("seq", "head")),
        check_vma=False,
    )
```

```python
import functools
import math

import jax
import jax.numpy as jnp
from jax import lax
from jax.experimental import pallas as pl
from jax.experimental.pallas import tpu as pltpu
from jax.sharding import PartitionSpec as P

INPUT_FEATURES = 2048
KEY_VALUE_HEADS = 4
HEAD_DIMENSION = 128
QUERY_PER_GROUP = 4


masked_score = -1e30
key_block = 512


def attend_fold(query_rows, query_pos, score_scale):
    head_size = query_rows.shape[1]

    def single_block(carry_state, block_rows, offset):
        running_max, row_total, context_sum = carry_state
        key_rows = block_rows[:, :head_size]
        value_rows = block_rows[:, head_size:].astype(jnp.float32)
        scores = jnp.dot(query_rows, key_rows.T, preferred_element_type=jnp.float32) * score_scale
        key_pos = offset + jnp.arange(block_rows.shape[0], dtype=jnp.int32)
        allowed = key_pos[None, :] <= query_pos[:, None]
        scores = jnp.where(allowed, scores, masked_score)
        new_max = jnp.maximum(running_max, jnp.max(scores, axis=1))
        factor = jnp.exp(running_max - new_max)
        weights = jnp.where(allowed, jnp.exp(scores - new_max[:, None]), 0.0)
        row_total = row_total * factor + jnp.sum(weights, axis=1)
        context_sum = context_sum * factor[:, None] + jnp.dot(
            weights, value_rows, precision=lax.Precision.HIGHEST, preferred_element_type=jnp.float32
        )
        return (new_max, row_total, context_sum)

    def fold_keys(carry_state, block_rows, offset):
        row_count = block_rows.shape[0]
        if row_count > key_block and row_count % key_block == 0:

            def sub_block(block_index, inner_state):
                part_rows = lax.dynamic_slice_in_dim(
                    block_rows, block_index * key_block, key_block, 0
                )
                return single_block(inner_state, part_rows, block_index * key_block)

            return lax.fori_loop(0, row_count // key_block, sub_block, carry_state)
        return single_block(carry_state, block_rows, offset)

    return fold_keys


def on_device(tokens, projection, context_cotangent):
    score_scale = HEAD_DIMENSION ** (-0.5)
    local_rows = tokens.shape[0]
    rows_all = local_rows * QUERY_PER_GROUP
    first_row = lax.axis_index("seq") * local_rows
    query_pos = first_row + jnp.arange(rows_all, dtype=jnp.int32) // QUERY_PER_GROUP

    def split_heads(projected_weight):
        reshaped_grads = projected_weight.reshape(local_rows, QUERY_PER_GROUP + 2, HEAD_DIMENSION)
        query_rows = reshaped_grads[:, :QUERY_PER_GROUP].reshape(rows_all, HEAD_DIMENSION)
        key_value = reshaped_grads[:, QUERY_PER_GROUP:].reshape(local_rows, 2 * HEAD_DIMENSION)
        return (query_rows, key_value)

    def empty_state():
        return (
            jnp.full((rows_all,), masked_score, jnp.float32),
            jnp.zeros((rows_all,), jnp.float32),
            jnp.zeros((rows_all, HEAD_DIMENSION), jnp.float32),
        )

    projected_weight = jnp.dot(tokens, projection, preferred_element_type=jnp.float32).astype(
        jnp.bfloat16
    )
    query_rows, key_value = split_heads(projected_weight)
    gathered = lax.all_gather(key_value, "seq", axis=0, tiled=True)
    total_rows = gathered.shape[0]
    block_size = min(key_block, total_rows)
    needed = (first_row + local_rows - 1) // block_size + 1
    fold_first = attend_fold(query_rows, query_pos, score_scale)

    def forward_step(block_index, carry_state):
        block_rows = lax.dynamic_slice_in_dim(gathered, block_index * block_size, block_size, 0)
        return fold_first(carry_state, block_rows, block_index * block_size)

    running_max, row_total, context_sum = lax.fori_loop(0, needed, forward_step, empty_state())
    context = (context_sum / row_total[:, None]).astype(jnp.bfloat16)
    log_total = running_max + jnp.log(row_total)
    grad_rows = context_cotangent.reshape(rows_all, HEAD_DIMENSION)
    row_delta = jnp.sum(grad_rows.astype(jnp.float32) * context.astype(jnp.float32), axis=1)
    contract_rows = (((0,), (0,)), ((), ()))

    def backward_step(block_index, carry_state):
        query_grad, key_terms = carry_state
        offset = block_index * block_size
        block_rows = lax.dynamic_slice_in_dim(gathered, offset, block_size, 0)
        key_rows = block_rows[:, :HEAD_DIMENSION]
        value_rows = block_rows[:, HEAD_DIMENSION:]
        scores = jnp.dot(query_rows, key_rows.T, preferred_element_type=jnp.float32) * score_scale
        key_pos = offset + jnp.arange(block_size, dtype=jnp.int32)
        allowed = key_pos[None, :] <= query_pos[:, None]
        probs_full = jnp.where(allowed, jnp.exp(scores - log_total[:, None]), 0.0)
        probs_half = probs_full.astype(jnp.bfloat16)
        prob_grad = jnp.dot(grad_rows, value_rows.T, preferred_element_type=jnp.float32)
        score_grad = (probs_full * (prob_grad - row_delta[:, None]) * score_scale).astype(
            jnp.bfloat16
        )
        query_grad = query_grad + jnp.dot(score_grad, key_rows, preferred_element_type=jnp.float32)
        key_grad = lax.dot_general(
            score_grad, query_rows, contract_rows, preferred_element_type=jnp.float32
        )
        value_grad = lax.dot_general(
            probs_half, grad_rows, contract_rows, preferred_element_type=jnp.float32
        )
        key_terms = lax.dynamic_update_slice_in_dim(
            key_terms, jnp.concatenate([key_grad, value_grad], axis=1), offset, 0
        )
        return (query_grad, key_terms)

    initial = (
        jnp.zeros((rows_all, HEAD_DIMENSION), jnp.float32),
        jnp.zeros((total_rows, 2 * HEAD_DIMENSION), jnp.float32),
    )
    query_grad, key_terms = lax.fori_loop(0, needed, backward_step, initial)
    key_value_grad = lax.psum_scatter(key_terms, "seq", scatter_dimension=0, tiled=True).astype(
        jnp.bfloat16
    )
    head_grads = jnp.concatenate(
        [
            query_grad.astype(jnp.bfloat16).reshape(local_rows, QUERY_PER_GROUP * HEAD_DIMENSION),
            key_value_grad,
        ],
        axis=1,
    )
    grad_term = lax.dot_general(
        tokens, head_grads, contract_rows, preferred_element_type=jnp.float32
    )
    normalizing_scale = math.sqrt(
        INPUT_FEATURES * KEY_VALUE_HEADS * (QUERY_PER_GROUP + 2) * HEAD_DIMENSION
    )
    ascent_radius = 0.2 * math.sqrt(KEY_VALUE_HEADS * (QUERY_PER_GROUP + 2) * HEAD_DIMENSION)
    weight_grad = lax.psum(grad_term, "seq")
    square_sum = lax.psum(jnp.sum(weight_grad * weight_grad), "head")
    grad_norm = jnp.sqrt(square_sum)
    share_rows = INPUT_FEATURES // lax.axis_size("seq")
    own_grad = lax.dynamic_slice_in_dim(
        weight_grad, lax.axis_index("seq") * share_rows, share_rows, 0
    )
    direction = own_grad * (normalizing_scale / grad_norm)
    moved_weights = (
        projection.astype(jnp.float32) + ascent_radius / grad_norm * weight_grad
    ).astype(jnp.bfloat16)
    projected_new = jnp.dot(tokens, moved_weights, preferred_element_type=jnp.float32).astype(
        jnp.bfloat16
    )
    query_new, key_value_new = split_heads(projected_new)
    fold_new = attend_fold(query_new, query_pos, score_scale)
    final_state = fold_new(
        empty_state(), lax.all_gather(key_value_new, "seq", axis=0, tiled=True), jnp.int32(0)
    )
    perturbed = (
        (final_state[2] / final_state[1][:, None])
        .astype(jnp.bfloat16)
        .reshape(local_rows, QUERY_PER_GROUP * HEAD_DIMENSION)
    )
    return (perturbed, direction)


CONTRACT_LAST = (((1,), (1,)), ((), ()))
CONTRACT_FIRST = (((0,), (0,)), ((), ()))
SCALE = HEAD_DIMENSION ** (-0.5)
SCALE_LOG2 = SCALE * math.log2(math.e)
QW = QUERY_PER_GROUP * HEAD_DIMENSION
D = HEAD_DIMENSION
VMEM_BUDGET = 60 * 1024 * 1024


def flip(index, mask):
    bit = 1
    while bit <= mask:
        if mask & bit:
            index = index + bit - 2 * bit * ((index // bit) % 2)
        bit *= 2
    return index


def resident_kernel(
    seq_size, radius, root, tokens_ref, cotangent_ref, projection_hbm, out, direction,
    tokens, cotangent, projection, projected, base_q, base_kv, key_t, value_t, grads,
    key_sum, value_sum, weight_half, own_grad, move_q, move_kv, norms,
    local_sem, load_sem, own_sent, own_sent_c, fold_sent, fold_sent_c, got, got_c,
    across_sent, pair_sent, relay_sent, across_got, pair_got, relay_got, norm_sent, norm_got,
):
    s = lax.axis_index("seq")
    h = lax.axis_index("head")
    local_rows = tokens_ref.shape[0]
    parts, total, width = tokens.shape
    tile = min(256, total)
    share = own_grad.shape[0]

    def rows_of(index):
        return pl.ds(pl.multiple_of(index * local_rows, local_rows), local_rows)

    def columns_of(index):
        return pl.ds(pl.multiple_of(index * width, width), width)

    def remote(source, target, send, receive, mask_s, mask_h):
        return pltpu.make_async_remote_copy(
            src_ref=source, dst_ref=target, send_sem=send, recv_sem=receive,
            device_id=(flip(s, mask_s), flip(h, mask_h)), device_id_type=pl.DeviceIdType.MESH,
        )

    load = pltpu.make_async_copy(projection_hbm, projection, load_sem)
    load.start()
    even = [k for k in range(2, seq_size, 2)]
    barrier = pltpu.get_barrier_semaphore()
    greeted = [(k, 0) for k in [1] + even] + [(0, q) for q in range(1, parts)]
    for mask_s, mask_h in greeted:
        pl.semaphore_signal(barrier, inc=1, device_id=(flip(s, mask_s), flip(h, mask_h)),
                            device_id_type=pl.DeviceIdType.MESH)
    pl.semaphore_wait(barrier, len(greeted))

    sent = []

    def send(source, target, send_sem, receive, mask_s, mask_h):
        copy = remote(source, target, send_sem, receive, mask_s, mask_h)
        copy.start()
        sent.append(copy)

    own_rows = rows_of(s)
    for k in even + [1]:
        send(tokens_ref.at[:, columns_of(h)], tokens.at[h, own_rows], own_sent.at[k], got.at[k],
             k, 0)
    for k in even + [1]:
        send(cotangent_ref, cotangent.at[own_rows], own_sent_c.at[k], got_c.at[k], k, 0)
    local = [pltpu.make_async_copy(tokens_ref.at[:, columns_of(q)], tokens.at[q, own_rows],
                                   local_sem.at[q]) for q in range(parts)]
    local.append(pltpu.make_async_copy(cotangent_ref, cotangent.at[own_rows],
                                       local_sem.at[parts]))
    for copy in local:
        copy.start()

    def token_rows(rows, weights, columns):
        acc = jnp.dot(tokens[0, rows, :], weights[pl.ds(0, width), columns],
                      preferred_element_type=jnp.float32)
        for q in range(1, parts):
            acc += jnp.dot(tokens[q, rows, :], weights[pl.ds(q * width, width), columns],
                           preferred_element_type=jnp.float32)
        return acc

    def project(k):
        rows = rows_of(flip(s, k))
        if k:
            place = tokens.at[flip(h, 1), rows]
            remote(place, place, own_sent.at[0], pair_got.at[k], 0, 1).wait_recv()
            place = tokens.at[flip(h, 3), rows]
            remote(place, place, own_sent.at[0], relay_got.at[k], 0, 1).wait_recv()
        acc = token_rows(rows, projection, slice(None))
        if k == 0:
            base_q[...] = acc[:, :QW]
        base_kv[rows, :] = acc[:, QW:]
        half = acc.astype(jnp.bfloat16)
        projected[rows, :] = half
        half_f = half.astype(jnp.float32)
        key_t[:, rows] = half_f[:, QW : QW + D].T.astype(jnp.bfloat16)
        value_t[:, rows] = half_f[:, QW + D :].T.astype(jnp.bfloat16)

    def arrived(k):
        place = tokens.at[h, rows_of(flip(s, k))]
        remote(place, place, own_sent.at[0], got.at[k], 1, 0).wait_recv()
        if k % 2 == 0:
            send(place, place, fold_sent.at[k], got.at[k + 1], 1, 0)
        send(place, place, across_sent.at[k], across_got.at[k], 0, 2)
        send(place, place, pair_sent.at[k], pair_got.at[k], 0, 1)

    def arrived_c(k):
        place = cotangent.at[rows_of(flip(s, k))]
        remote(place, place, own_sent.at[0], got_c.at[k], 1, 0).wait_recv()
        if k % 2 == 0:
            send(place, place, fold_sent_c.at[k], got_c.at[k + 1], 1, 0)

    def relay(k):
        place = tokens.at[flip(h, 2), rows_of(flip(s, k))]
        remote(place, place, own_sent.at[0], across_got.at[k], 0, 2).wait_recv()
        send(place, place, relay_sent.at[k], relay_got.at[k], 0, 1)

    for copy in local:
        copy.wait()
    load.wait()

    order = [even[0], 1] + [k for j in even[1:] for k in (j, )] + [k + 1 for k in even]
    project_queue = [0] + order
    for position, k in enumerate(order):
        arrived(k)
        if position >= 1:
            relay(order[position - 1])
        if position == 1:
            project(project_queue.pop(0))
        if position >= 4:
            project(project_queue.pop(0))
    relay(order[-1])
    for k in even:
        arrived_c(k)
        project(project_queue.pop(0))
    while project_queue:
        project(project_queue.pop(0))
    for k in order:
        if k % 2:
            arrived_c(k)

    key_sum[...] = jnp.zeros_like(key_sum)
    value_sum[...] = jnp.zeros_like(value_sum)

    allowed = lax.broadcasted_iota(jnp.int32, (tile, tile), 0) <= lax.broadcasted_iota(
        jnp.int32, (tile, tile), 1
    )
    for block in range(total // tile):
        length = (block + 1) * tile
        rows = slice(block * tile, length)

        @pl.loop(0, QUERY_PER_GROUP)
        def _(head):
            columns = pl.ds(pl.multiple_of(head * D, D), D)
            query = projected[rows, columns]
            out_grad = cotangent[rows, columns]
            scores = lax.dot_general(projected[:length, QW : QW + D], query, CONTRACT_LAST,
                                     preferred_element_type=jnp.float32)
            last = jnp.where(allowed, scores[block * tile :], masked_score)
            scores = last if block == 0 else jnp.concatenate([scores[: block * tile], last], 0)
            top = jnp.max(scores, axis=0, keepdims=True)
            weights = jnp.exp2(scores * SCALE_LOG2 - top * SCALE_LOG2)
            probs = weights * (1.0 / jnp.sum(weights, axis=0, keepdims=True))
            probs_half = probs.astype(jnp.bfloat16)
            context_t = jnp.dot(value_t[:, :length], probs_half,
                                preferred_element_type=jnp.float32)
            context_t = context_t.astype(jnp.bfloat16).astype(jnp.float32)
            delta = jnp.sum(out_grad.astype(jnp.float32).T * context_t, axis=0, keepdims=True)
            prob_grad = lax.dot_general(projected[:length, QW + D :], out_grad, CONTRACT_LAST,
                                        preferred_element_type=jnp.float32)
            score_grad = (probs * (prob_grad - delta)).astype(jnp.bfloat16)
            query_t = jnp.dot(key_t[:, :length], score_grad, preferred_element_type=jnp.float32)
            grads[rows, columns] = (query_t * SCALE).T.astype(jnp.bfloat16)
            key_sum[:length, :] += jnp.dot(score_grad, query, preferred_element_type=jnp.float32)
            value_sum[:length, :] += jnp.dot(probs_half, out_grad,
                                             preferred_element_type=jnp.float32)

    grads[:, QW : QW + D] = (key_sum[...] * SCALE).astype(jnp.bfloat16)
    grads[:, QW + D :] = value_sum[...].astype(jnp.bfloat16)

    per_part = width // share
    norms[0] = jnp.zeros_like(norms[0])

    @pl.loop(0, parts * per_part)
    def _(chunk):
        columns = pl.ds(pl.multiple_of((chunk % per_part) * share, share), share)
        rows = pl.ds(pl.multiple_of(chunk * share, share), share)
        block = lax.dot_general(tokens[chunk // per_part, :, columns], grads[...], CONTRACT_FIRST,
                                preferred_element_type=jnp.float32)
        squared = block * block
        lanes = squared[:, :128]
        for start in range(128, squared.shape[1], 128):
            lanes += squared[:, start : start + 128]
        norms[0] += jnp.sum(lanes.reshape(share // 8, 8, 128), axis=0)
        weight_half[rows, :] = block.astype(jnp.bfloat16)

        @pl.when(chunk == s)
        def _():
            own_grad[...] = block

    move_q[...] = token_rows(own_rows, weight_half, slice(0, QW))
    for q in range(1, parts):
        send(norms.at[0], norms.at[q], norm_sent.at[q], norm_got.at[q], 0, q)

    @pl.loop(0, total // tile)
    def _(block):
        rows = pl.ds(pl.multiple_of(block * tile, tile), tile)
        move_kv[rows, :] = token_rows(rows, weight_half, slice(QW, None))

    for q in range(1, parts):
        remote(norms.at[q], norms.at[q], norm_sent.at[0], norm_got.at[q], 0, q).wait_recv()
    square_sum = jnp.sum(jnp.sum(norms[...], axis=0), keepdims=True)
    inverse = 1.0 / jnp.sqrt(square_sum)
    direction[...] = own_grad[...] * (root * inverse)
    step_size = radius * inverse
    query = (base_q[...] + step_size * move_q[...]).astype(jnp.bfloat16)
    key_value = (base_kv[...] + step_size * move_kv[...]).astype(jnp.bfloat16)
    new_value_t = key_value[:, D:].astype(jnp.float32).T.astype(jnp.bfloat16)
    stacked = jnp.concatenate(
        [query[:, g * D : (g + 1) * D] for g in range(QUERY_PER_GROUP)], axis=0
    )
    scores = lax.dot_general(key_value[:, :D], stacked, CONTRACT_LAST,
                             preferred_element_type=jnp.float32)
    key_pos = lax.broadcasted_iota(jnp.int32, (total, local_rows), 0)
    row_pos = lax.broadcasted_iota(jnp.int32, (total, local_rows), 1) + s * local_rows
    visible = key_pos <= row_pos
    for g in range(QUERY_PER_GROUP):
        part = jnp.where(visible, scores[:, g * local_rows : (g + 1) * local_rows], masked_score)
        top = jnp.max(part, axis=0, keepdims=True)
        weights = jnp.exp2(part * SCALE_LOG2 - top * SCALE_LOG2)
        sums = jnp.sum(weights, axis=0, keepdims=True)
        context_t = jnp.dot(new_value_t, weights.astype(jnp.bfloat16),
                            preferred_element_type=jnp.float32) / sums
        out[:, g * D : (g + 1) * D] = context_t.T.astype(jnp.bfloat16)
    for copy in sent:
        copy.wait_send()


def resident_step(tokens, projection, cotangent):
    seq_size, parts = lax.axis_size("seq"), lax.axis_size("head")
    local_rows, features = tokens.shape
    columns = projection.shape[1]
    share = features // seq_size
    total = local_rows * seq_size
    f32, bf16 = jnp.float32, jnp.bfloat16
    root = math.sqrt(features * parts * columns)
    radius = 0.2 * math.sqrt(parts * columns)
    in_vmem = pl.BlockSpec(memory_space=pltpu.VMEM)
    return pl.pallas_call(
        functools.partial(resident_kernel, seq_size, radius, root),
        out_shape=(
            jax.ShapeDtypeStruct((local_rows, QW), bf16),
            jax.ShapeDtypeStruct((share, columns), f32),
        ),
        in_specs=[in_vmem, in_vmem, pl.BlockSpec(memory_space=pl.ANY)],
        out_specs=(in_vmem, in_vmem),
        scratch_shapes=[
            pltpu.VMEM((parts, total, features // parts), bf16),
            pltpu.VMEM((total, QW), bf16),
            pltpu.VMEM((features, columns), bf16),
            pltpu.VMEM((total, columns), bf16),
            pltpu.VMEM((local_rows, QW), f32),
            pltpu.VMEM((total, 2 * D), f32),
            pltpu.VMEM((D, total), bf16),
            pltpu.VMEM((D, total), bf16),
            pltpu.VMEM((total, columns), bf16),
            pltpu.VMEM((total, D), f32),
            pltpu.VMEM((total, D), f32),
            pltpu.VMEM((features, columns), bf16),
            pltpu.VMEM((share, columns), f32),
            pltpu.VMEM((local_rows, QW), f32),
            pltpu.VMEM((total, 2 * D), f32),
            pltpu.VMEM((parts, 8, 128), f32),
            pltpu.SemaphoreType.DMA((parts + 1,)),
            pltpu.SemaphoreType.DMA,
        ]
        + [pltpu.SemaphoreType.DMA((seq_size,))] * 12
        + [pltpu.SemaphoreType.DMA((parts,))] * 2,
        compiler_params=pltpu.CompilerParams(
            collective_id=0, has_side_effects=True, vmem_limit_bytes=VMEM_BUDGET
        ),
        name="resident",
    )(tokens, cotangent, projection)


def fits(local_rows, features, columns, seq_size, head_size):
    total = local_rows * seq_size
    share = features // seq_size
    held = total * (2 * features + 2 * QW + 12 * columns + 24 * D) + 4 * features * columns
    pairs = seq_size >= 4 and seq_size & (seq_size - 1) == 0 and head_size == 4
    aligned = share % 128 == 0 and (features // head_size) % share == 0 and local_rows % 128 == 0
    return pairs and aligned and held < VMEM_BUDGET // 2


def step(tokens, projection, context_cotangent):
    sizes = (*tokens.shape, projection.shape[1], lax.axis_size("seq"), lax.axis_size("head"))
    if fits(*sizes):
        return resident_step(tokens, projection, context_cotangent)
    return on_device(tokens, projection, context_cotangent)


def solution(mesh):
    return jax.shard_map(
        step,
        mesh=mesh,
        in_specs=(P("seq", None), P(None, "head"), P("seq", "head")),
        out_specs=(P("seq", "head"), P("seq", "head")),
        check_vma=False,
    )
```

```python
import functools
import math

import jax
import jax.numpy as jnp
from jax import lax
from jax.experimental import pallas as pl
from jax.experimental.pallas import tpu as pltpu
from jax.sharding import PartitionSpec as P

INPUT_FEATURES = 2048
KEY_VALUE_HEADS = 4
HEAD_DIMENSION = 128
QUERY_PER_GROUP = 4


masked_score = -1e30
key_block = 512


def attend_fold(query_rows, query_pos, score_scale):
    head_size = query_rows.shape[1]

    def single_block(carry_state, block_rows, offset):
        running_max, row_total, context_sum = carry_state
        key_rows = block_rows[:, :head_size]
        value_rows = block_rows[:, head_size:].astype(jnp.float32)
        scores = jnp.dot(query_rows, key_rows.T, preferred_element_type=jnp.float32) * score_scale
        key_pos = offset + jnp.arange(block_rows.shape[0], dtype=jnp.int32)
        allowed = key_pos[None, :] <= query_pos[:, None]
        scores = jnp.where(allowed, scores, masked_score)
        new_max = jnp.maximum(running_max, jnp.max(scores, axis=1))
        factor = jnp.exp(running_max - new_max)
        weights = jnp.where(allowed, jnp.exp(scores - new_max[:, None]), 0.0)
        row_total = row_total * factor + jnp.sum(weights, axis=1)
        context_sum = context_sum * factor[:, None] + jnp.dot(
            weights, value_rows, precision=lax.Precision.HIGHEST, preferred_element_type=jnp.float32
        )
        return (new_max, row_total, context_sum)

    def fold_keys(carry_state, block_rows, offset):
        row_count = block_rows.shape[0]
        if row_count > key_block and row_count % key_block == 0:

            def sub_block(block_index, inner_state):
                part_rows = lax.dynamic_slice_in_dim(
                    block_rows, block_index * key_block, key_block, 0
                )
                return single_block(inner_state, part_rows, block_index * key_block)

            return lax.fori_loop(0, row_count // key_block, sub_block, carry_state)
        return single_block(carry_state, block_rows, offset)

    return fold_keys


def on_device(tokens, projection, context_cotangent):
    score_scale = HEAD_DIMENSION ** (-0.5)
    local_rows = tokens.shape[0]
    rows_all = local_rows * QUERY_PER_GROUP
    first_row = lax.axis_index("seq") * local_rows
    query_pos = first_row + jnp.arange(rows_all, dtype=jnp.int32) // QUERY_PER_GROUP

    def split_heads(projected_weight):
        reshaped_grads = projected_weight.reshape(local_rows, QUERY_PER_GROUP + 2, HEAD_DIMENSION)
        query_rows = reshaped_grads[:, :QUERY_PER_GROUP].reshape(rows_all, HEAD_DIMENSION)
        key_value = reshaped_grads[:, QUERY_PER_GROUP:].reshape(local_rows, 2 * HEAD_DIMENSION)
        return (query_rows, key_value)

    def empty_state():
        return (
            jnp.full((rows_all,), masked_score, jnp.float32),
            jnp.zeros((rows_all,), jnp.float32),
            jnp.zeros((rows_all, HEAD_DIMENSION), jnp.float32),
        )

    projected_weight = jnp.dot(tokens, projection, preferred_element_type=jnp.float32).astype(
        jnp.bfloat16
    )
    query_rows, key_value = split_heads(projected_weight)
    gathered = lax.all_gather(key_value, "seq", axis=0, tiled=True)
    total_rows = gathered.shape[0]
    block_size = min(key_block, total_rows)
    needed = (first_row + local_rows - 1) // block_size + 1
    fold_first = attend_fold(query_rows, query_pos, score_scale)

    def forward_step(block_index, carry_state):
        block_rows = lax.dynamic_slice_in_dim(gathered, block_index * block_size, block_size, 0)
        return fold_first(carry_state, block_rows, block_index * block_size)

    running_max, row_total, context_sum = lax.fori_loop(0, needed, forward_step, empty_state())
    context = (context_sum / row_total[:, None]).astype(jnp.bfloat16)
    log_total = running_max + jnp.log(row_total)
    grad_rows = context_cotangent.reshape(rows_all, HEAD_DIMENSION)
    row_delta = jnp.sum(grad_rows.astype(jnp.float32) * context.astype(jnp.float32), axis=1)
    contract_rows = (((0,), (0,)), ((), ()))

    def backward_step(block_index, carry_state):
        query_grad, key_terms = carry_state
        offset = block_index * block_size
        block_rows = lax.dynamic_slice_in_dim(gathered, offset, block_size, 0)
        key_rows = block_rows[:, :HEAD_DIMENSION]
        value_rows = block_rows[:, HEAD_DIMENSION:]
        scores = jnp.dot(query_rows, key_rows.T, preferred_element_type=jnp.float32) * score_scale
        key_pos = offset + jnp.arange(block_size, dtype=jnp.int32)
        allowed = key_pos[None, :] <= query_pos[:, None]
        probs_full = jnp.where(allowed, jnp.exp(scores - log_total[:, None]), 0.0)
        probs_half = probs_full.astype(jnp.bfloat16)
        prob_grad = jnp.dot(grad_rows, value_rows.T, preferred_element_type=jnp.float32)
        score_grad = (probs_full * (prob_grad - row_delta[:, None]) * score_scale).astype(
            jnp.bfloat16
        )
        query_grad = query_grad + jnp.dot(score_grad, key_rows, preferred_element_type=jnp.float32)
        key_grad = lax.dot_general(
            score_grad, query_rows, contract_rows, preferred_element_type=jnp.float32
        )
        value_grad = lax.dot_general(
            probs_half, grad_rows, contract_rows, preferred_element_type=jnp.float32
        )
        key_terms = lax.dynamic_update_slice_in_dim(
            key_terms, jnp.concatenate([key_grad, value_grad], axis=1), offset, 0
        )
        return (query_grad, key_terms)

    initial = (
        jnp.zeros((rows_all, HEAD_DIMENSION), jnp.float32),
        jnp.zeros((total_rows, 2 * HEAD_DIMENSION), jnp.float32),
    )
    query_grad, key_terms = lax.fori_loop(0, needed, backward_step, initial)
    key_value_grad = lax.psum_scatter(key_terms, "seq", scatter_dimension=0, tiled=True).astype(
        jnp.bfloat16
    )
    head_grads = jnp.concatenate(
        [
            query_grad.astype(jnp.bfloat16).reshape(local_rows, QUERY_PER_GROUP * HEAD_DIMENSION),
            key_value_grad,
        ],
        axis=1,
    )
    grad_term = lax.dot_general(
        tokens, head_grads, contract_rows, preferred_element_type=jnp.float32
    )
    normalizing_scale = math.sqrt(
        INPUT_FEATURES * KEY_VALUE_HEADS * (QUERY_PER_GROUP + 2) * HEAD_DIMENSION
    )
    ascent_radius = 0.2 * math.sqrt(KEY_VALUE_HEADS * (QUERY_PER_GROUP + 2) * HEAD_DIMENSION)
    weight_grad = lax.psum(grad_term, "seq")
    square_sum = lax.psum(jnp.sum(weight_grad * weight_grad), "head")
    grad_norm = jnp.sqrt(square_sum)
    share_rows = INPUT_FEATURES // lax.axis_size("seq")
    own_grad = lax.dynamic_slice_in_dim(
        weight_grad, lax.axis_index("seq") * share_rows, share_rows, 0
    )
    direction = own_grad * (normalizing_scale / grad_norm)
    moved_weights = (
        projection.astype(jnp.float32) + ascent_radius / grad_norm * weight_grad
    ).astype(jnp.bfloat16)
    projected_new = jnp.dot(tokens, moved_weights, preferred_element_type=jnp.float32).astype(
        jnp.bfloat16
    )
    query_new, key_value_new = split_heads(projected_new)
    fold_new = attend_fold(query_new, query_pos, score_scale)
    final_state = fold_new(
        empty_state(), lax.all_gather(key_value_new, "seq", axis=0, tiled=True), jnp.int32(0)
    )
    perturbed = (
        (final_state[2] / final_state[1][:, None])
        .astype(jnp.bfloat16)
        .reshape(local_rows, QUERY_PER_GROUP * HEAD_DIMENSION)
    )
    return (perturbed, direction)


CONTRACT_LAST = (((1,), (1,)), ((), ()))
CONTRACT_FIRST = (((0,), (0,)), ((), ()))
SCALE = HEAD_DIMENSION ** (-0.5)
SCALE_LOG2 = SCALE * math.log2(math.e)
QW = QUERY_PER_GROUP * HEAD_DIMENSION
D = HEAD_DIMENSION
VMEM_BUDGET = 60 * 1024 * 1024


def flip(index, mask):
    bit = 1
    while bit <= mask:
        if mask & bit:
            index = index + bit - 2 * bit * ((index // bit) % 2)
        bit *= 2
    return index


def resident_kernel(
    seq_size, radius, root, tokens_ref, cotangent_ref, projection_hbm, out, direction,
    tokens, cotangent, projection, projected, base_q, base_kv, key_t, value_t, grads,
    key_sum, value_sum, weight_half, own_grad, move_q, move_kv, norms,
    local_sem, load_sem, own_sent, own_sent_c, line_sent, line_sent_c, fold_sent, fold_sent_c,
    got, got_c, across_sent, pair_sent, relay_sent, across_got, pair_got, relay_got,
    norm_sent, norm_got,
):
    s = lax.axis_index("seq")
    h = lax.axis_index("head")
    local_rows = tokens_ref.shape[0]
    parts, total, width = tokens.shape
    tile = min(256, total)
    share = own_grad.shape[0]

    def rows_of(index):
        return pl.ds(pl.multiple_of(index * local_rows, local_rows), local_rows)

    def columns_of(index):
        return pl.ds(pl.multiple_of(index * width, width), width)

    mesh_type = pl.DeviceIdType.MESH
    partner = flip(s, 1)
    side = s % 2
    place_on_line = s // 2
    length_of_line = seq_size // 2
    has_right = place_on_line < length_of_line - 1
    has_left = place_on_line > 0

    def remote(source, target, send, receive, to_s, to_h):
        return pltpu.make_async_remote_copy(
            src_ref=source, dst_ref=target, send_sem=send, recv_sem=receive,
            device_id=(to_s, to_h), device_id_type=mesh_type,
        )

    def line_block(j):
        near = jnp.minimum(place_on_line, length_of_line - 1 - place_on_line)
        alternate = place_on_line - 1 - j // 2 if j % 2 == 0 else place_on_line + 1 + j // 2
        beyond = jnp.where(place_on_line > near, length_of_line - 2 - j, j + 1)
        return jnp.where(j < 2 * near, alternate, beyond)

    load = pltpu.make_async_copy(projection_hbm, projection, load_sem)
    load.start()
    barrier = pltpu.get_barrier_semaphore()

    def greet(to_s, to_h):
        pl.semaphore_signal(barrier, inc=1, device_id=(to_s, to_h), device_id_type=mesh_type)

    greet(partner, h)
    for q in range(1, parts):
        greet(s, flip(h, q))

    @pl.when(has_right)
    def _():
        greet(s + 2, h)

    @pl.when(has_left)
    def _():
        greet(s - 2, h)

    both_sides = jnp.minimum(place_on_line, 1) + jnp.minimum(length_of_line - 1 - place_on_line, 1)
    pl.semaphore_wait(barrier, parts + both_sides)

    sent = []

    def send(source, target, send_sem, receive, to_s, to_h, when=None):
        copy = remote(source, target, send_sem, receive, to_s, to_h)
        sent.append((copy, when))
        if when is None:
            copy.start()
        else:

            @pl.when(when)
            def _():
                copy.start()

    own_rows = rows_of(s)

    def send_own(source, place, send_sem, receive):
        send(source, place, send_sem.at[0], receive.at[s], s + 2, h, has_right)
        send(source, place, send_sem.at[1], receive.at[s], s - 2, h, has_left)
        send(source, place, send_sem.at[2], receive.at[s], partner, h)

    send_own(tokens_ref.at[:, columns_of(h)], tokens.at[h, own_rows], own_sent, got)
    local = [pltpu.make_async_copy(tokens_ref.at[:, columns_of(q)], tokens.at[q, own_rows],
                                   local_sem.at[q]) for q in range(parts)]
    local.append(pltpu.make_async_copy(cotangent_ref, cotangent.at[own_rows],
                                       local_sem.at[parts]))
    for copy in local:
        copy.start()

    def token_rows(rows, weights, columns):
        acc = jnp.dot(tokens[0, rows, :], weights[pl.ds(0, width), columns],
                      preferred_element_type=jnp.float32)
        for q in range(1, parts):
            acc += jnp.dot(tokens[q, rows, :], weights[pl.ds(q * width, width), columns],
                           preferred_element_type=jnp.float32)
        return acc

    def index_of(kind, j):
        if kind == "own":
            return s
        if kind == "pair":
            return partner
        return line_block(j) * 2 + (side if kind == "line" else 1 - side)

    def wait_for(place, semaphore):
        remote(place, place, own_sent.at[2], semaphore, partner, h).wait_recv()

    def project(kind, j=0):
        index = index_of(kind, j)
        rows = rows_of(index)
        if kind != "own":
            wait_for(tokens.at[flip(h, 1), rows], pair_got.at[index])
            wait_for(tokens.at[flip(h, 3), rows], relay_got.at[index])
        acc = token_rows(rows, projection, slice(None))
        if kind == "own":
            base_q[...] = acc[:, :QW]
        base_kv[rows, :] = acc[:, QW:]
        half = acc.astype(jnp.bfloat16)
        projected[rows, :] = half
        half_f = half.astype(jnp.float32)
        key_t[:, rows] = half_f[:, QW : QW + D].T.astype(jnp.bfloat16)
        value_t[:, rows] = half_f[:, QW + D :].T.astype(jnp.bfloat16)

    def pass_on(place, index, line, fold, receive):
        ahead = index // 2 < place_on_line
        to_s = jnp.where(ahead, s + 2, s - 2)
        more = jnp.where(ahead, place_on_line < length_of_line - 1, place_on_line > 0)
        send(place, place, line.at[index], receive.at[index], to_s, h, more)
        send(place, place, fold.at[index], receive.at[index], partner, h)

    def arrived(kind, j=0):
        index = index_of(kind, j)
        place = tokens.at[h, rows_of(index)]
        wait_for(place, got.at[index])
        if kind == "line":
            pass_on(place, index, line_sent, fold_sent, got)
        send(place, place, across_sent.at[index], across_got.at[index], s, flip(h, 2))
        send(place, place, pair_sent.at[index], pair_got.at[index], s, flip(h, 1))

    def arrived_c(kind, j=0):
        index = index_of(kind, j)
        place = cotangent.at[rows_of(index)]
        wait_for(place, got_c.at[index])
        if kind == "line":
            pass_on(place, index, line_sent_c, fold_sent_c, got_c)

    def relay(kind, j=0):
        index = index_of(kind, j)
        place = tokens.at[flip(h, 2), rows_of(index)]
        wait_for(place, across_got.at[index])
        send(place, place, relay_sent.at[index], relay_got.at[index], s, flip(h, 1))

    for copy in local:
        copy.wait()

    steps = length_of_line - 1
    order = [("line", 0), ("pair", 0)]
    for j in range(1, steps):
        order += [("line", j), ("fold", j - 1)]
    order.append(("fold", steps - 1))
    queue = [("own", 0)] + order
    cotangents = [("line", j) for j in range(steps)]
    for position, item in enumerate(order):
        arrived(*item)
        if item == ("line", 1):
            send_own(cotangent_ref, cotangent.at[own_rows], own_sent_c, got_c)
        if position == 3:
            load.wait()
        if position >= 3:
            relay(*order[position - 3])
            project(*queue.pop(0))
        if position >= 5 and cotangents:
            arrived_c(*cotangents.pop(0))
    for item in order[-3:]:
        if cotangents:
            arrived_c(*cotangents.pop(0))
        relay(*item)
        project(*queue.pop(0))
    while cotangents:
        arrived_c(*cotangents.pop(0))
    while queue:
        project(*queue.pop(0))
    arrived_c("pair")
    for j in range(steps):
        arrived_c("fold", j)

    key_sum[...] = jnp.zeros_like(key_sum)
    value_sum[...] = jnp.zeros_like(value_sum)

    allowed = lax.broadcasted_iota(jnp.int32, (tile, tile), 0) <= lax.broadcasted_iota(
        jnp.int32, (tile, tile), 1
    )
    for block in range(total // tile):
        length = (block + 1) * tile
        rows = slice(block * tile, length)

        @pl.loop(0, QUERY_PER_GROUP)
        def _(head):
            columns = pl.ds(pl.multiple_of(head * D, D), D)
            query = projected[rows, columns]
            out_grad = cotangent[rows, columns]
            scores = lax.dot_general(projected[:length, QW : QW + D], query, CONTRACT_LAST,
                                     preferred_element_type=jnp.float32)
            last = jnp.where(allowed, scores[block * tile :], masked_score)
            scores = last if block == 0 else jnp.concatenate([scores[: block * tile], last], 0)
            top = jnp.max(scores, axis=0, keepdims=True)
            weights = jnp.exp2(scores * SCALE_LOG2 - top * SCALE_LOG2)
            probs = weights * (1.0 / jnp.sum(weights, axis=0, keepdims=True))
            probs_half = probs.astype(jnp.bfloat16)
            context_t = jnp.dot(value_t[:, :length], probs_half,
                                preferred_element_type=jnp.float32)
            context_t = context_t.astype(jnp.bfloat16).astype(jnp.float32)
            delta = jnp.sum(out_grad.astype(jnp.float32).T * context_t, axis=0, keepdims=True)
            prob_grad = lax.dot_general(projected[:length, QW + D :], out_grad, CONTRACT_LAST,
                                        preferred_element_type=jnp.float32)
            score_grad = (probs * (prob_grad - delta)).astype(jnp.bfloat16)
            query_t = jnp.dot(key_t[:, :length], score_grad, preferred_element_type=jnp.float32)
            grads[rows, columns] = (query_t * SCALE).T.astype(jnp.bfloat16)
            key_sum[:length, :] += jnp.dot(score_grad, query, preferred_element_type=jnp.float32)
            value_sum[:length, :] += jnp.dot(probs_half, out_grad,
                                             preferred_element_type=jnp.float32)

    grads[:, QW : QW + D] = (key_sum[...] * SCALE).astype(jnp.bfloat16)
    grads[:, QW + D :] = value_sum[...].astype(jnp.bfloat16)

    per_part = width // share
    norms[0] = jnp.zeros_like(norms[0])

    @pl.loop(0, parts * per_part)
    def _(chunk):
        columns = pl.ds(pl.multiple_of((chunk % per_part) * share, share), share)
        rows = pl.ds(pl.multiple_of(chunk * share, share), share)
        block = lax.dot_general(tokens[chunk // per_part, :, columns], grads[...], CONTRACT_FIRST,
                                preferred_element_type=jnp.float32)
        squared = block * block
        lanes = squared[:, :128]
        for start in range(128, squared.shape[1], 128):
            lanes += squared[:, start : start + 128]
        norms[0] += jnp.sum(lanes.reshape(share // 8, 8, 128), axis=0)
        weight_half[rows, :] = block.astype(jnp.bfloat16)

        @pl.when(chunk == s)
        def _():
            own_grad[...] = block

    move_q[...] = token_rows(own_rows, weight_half, slice(0, QW))
    for q in range(1, parts):
        send(norms.at[0], norms.at[q], norm_sent.at[q], norm_got.at[q], s, flip(h, q))

    @pl.loop(0, total // tile)
    def _(block):
        rows = pl.ds(pl.multiple_of(block * tile, tile), tile)
        move_kv[rows, :] = token_rows(rows, weight_half, slice(QW, None))

    for q in range(1, parts):
        remote(norms.at[q], norms.at[q], norm_sent.at[0], norm_got.at[q], s, flip(h, q)).wait_recv()
    square_sum = jnp.sum(jnp.sum(norms[...], axis=0), keepdims=True)
    inverse = 1.0 / jnp.sqrt(square_sum)
    direction[...] = own_grad[...] * (root * inverse)
    step_size = radius * inverse
    query = (base_q[...] + step_size * move_q[...]).astype(jnp.bfloat16)
    key_value = (base_kv[...] + step_size * move_kv[...]).astype(jnp.bfloat16)
    new_value_t = key_value[:, D:].astype(jnp.float32).T.astype(jnp.bfloat16)
    stacked = jnp.concatenate(
        [query[:, g * D : (g + 1) * D] for g in range(QUERY_PER_GROUP)], axis=0
    )
    scores = lax.dot_general(key_value[:, :D], stacked, CONTRACT_LAST,
                             preferred_element_type=jnp.float32)
    key_pos = lax.broadcasted_iota(jnp.int32, (total, local_rows), 0)
    row_pos = lax.broadcasted_iota(jnp.int32, (total, local_rows), 1) + s * local_rows
    visible = key_pos <= row_pos
    for g in range(QUERY_PER_GROUP):
        part = jnp.where(visible, scores[:, g * local_rows : (g + 1) * local_rows], masked_score)
        top = jnp.max(part, axis=0, keepdims=True)
        weights = jnp.exp2(part * SCALE_LOG2 - top * SCALE_LOG2)
        sums = jnp.sum(weights, axis=0, keepdims=True)
        context_t = jnp.dot(new_value_t, weights.astype(jnp.bfloat16),
                            preferred_element_type=jnp.float32) / sums
        out[:, g * D : (g + 1) * D] = context_t.T.astype(jnp.bfloat16)
    for copy, when in sent:
        if when is None:
            copy.wait_send()
        else:

            @pl.when(when)
            def _():
                copy.wait_send()


def resident_step(tokens, projection, cotangent):
    seq_size, parts = lax.axis_size("seq"), lax.axis_size("head")
    local_rows, features = tokens.shape
    columns = projection.shape[1]
    share = features // seq_size
    total = local_rows * seq_size
    f32, bf16 = jnp.float32, jnp.bfloat16
    root = math.sqrt(features * parts * columns)
    radius = 0.2 * math.sqrt(parts * columns)
    in_vmem = pl.BlockSpec(memory_space=pltpu.VMEM)
    return pl.pallas_call(
        functools.partial(resident_kernel, seq_size, radius, root),
        out_shape=(
            jax.ShapeDtypeStruct((local_rows, QW), bf16),
            jax.ShapeDtypeStruct((share, columns), f32),
        ),
        in_specs=[in_vmem, in_vmem, pl.BlockSpec(memory_space=pl.ANY)],
        out_specs=(in_vmem, in_vmem),
        scratch_shapes=[
            pltpu.VMEM((parts, total, features // parts), bf16),
            pltpu.VMEM((total, QW), bf16),
            pltpu.VMEM((features, columns), bf16),
            pltpu.VMEM((total, columns), bf16),
            pltpu.VMEM((local_rows, QW), f32),
            pltpu.VMEM((total, 2 * D), f32),
            pltpu.VMEM((D, total), bf16),
            pltpu.VMEM((D, total), bf16),
            pltpu.VMEM((total, columns), bf16),
            pltpu.VMEM((total, D), f32),
            pltpu.VMEM((total, D), f32),
            pltpu.VMEM((features, columns), bf16),
            pltpu.VMEM((share, columns), f32),
            pltpu.VMEM((local_rows, QW), f32),
            pltpu.VMEM((total, 2 * D), f32),
            pltpu.VMEM((parts, 8, 128), f32),
            pltpu.SemaphoreType.DMA((parts + 1,)),
            pltpu.SemaphoreType.DMA,
        ]
        + [pltpu.SemaphoreType.DMA((seq_size,))] * 14
        + [pltpu.SemaphoreType.DMA((parts,))] * 2,
        compiler_params=pltpu.CompilerParams(
            collective_id=0, has_side_effects=True, vmem_limit_bytes=VMEM_BUDGET
        ),
        name="resident",
    )(tokens, cotangent, projection)


def fits(local_rows, features, columns, seq_size, head_size):
    total = local_rows * seq_size
    share = features // seq_size
    held = total * (2 * features + 2 * QW + 12 * columns + 24 * D) + 4 * features * columns
    pairs = seq_size >= 8 and seq_size & (seq_size - 1) == 0 and head_size == 4
    aligned = share % 128 == 0 and (features // head_size) % share == 0 and local_rows % 128 == 0
    return pairs and aligned and held < VMEM_BUDGET // 2


def step(tokens, projection, context_cotangent):
    sizes = (*tokens.shape, projection.shape[1], lax.axis_size("seq"), lax.axis_size("head"))
    if fits(*sizes):
        return resident_step(tokens, projection, context_cotangent)
    return on_device(tokens, projection, context_cotangent)


def solution(mesh):
    return jax.shard_map(
        step,
        mesh=mesh,
        in_specs=(P("seq", None), P(None, "head"), P("seq", "head")),
        out_specs=(P("seq", "head"), P("seq", "head")),
        check_vma=False,
    )
```

```python
import functools
import math

import jax
import jax.numpy as jnp
from jax import lax
from jax.experimental import pallas as pl
from jax.experimental.pallas import tpu as pltpu
from jax.sharding import PartitionSpec as P

INPUT_FEATURES = 2048
KEY_VALUE_HEADS = 4
HEAD_DIMENSION = 128
QUERY_PER_GROUP = 4


masked_score = -1e30
key_block = 512


def attend_fold(query_rows, query_pos, score_scale):
    head_size = query_rows.shape[1]

    def single_block(carry_state, block_rows, offset):
        running_max, row_total, context_sum = carry_state
        key_rows = block_rows[:, :head_size]
        value_rows = block_rows[:, head_size:].astype(jnp.float32)
        scores = jnp.dot(query_rows, key_rows.T, preferred_element_type=jnp.float32) * score_scale
        key_pos = offset + jnp.arange(block_rows.shape[0], dtype=jnp.int32)
        allowed = key_pos[None, :] <= query_pos[:, None]
        scores = jnp.where(allowed, scores, masked_score)
        new_max = jnp.maximum(running_max, jnp.max(scores, axis=1))
        factor = jnp.exp(running_max - new_max)
        weights = jnp.where(allowed, jnp.exp(scores - new_max[:, None]), 0.0)
        row_total = row_total * factor + jnp.sum(weights, axis=1)
        context_sum = context_sum * factor[:, None] + jnp.dot(
            weights, value_rows, precision=lax.Precision.HIGHEST, preferred_element_type=jnp.float32
        )
        return (new_max, row_total, context_sum)

    def fold_keys(carry_state, block_rows, offset):
        row_count = block_rows.shape[0]
        if row_count > key_block and row_count % key_block == 0:

            def sub_block(block_index, inner_state):
                part_rows = lax.dynamic_slice_in_dim(
                    block_rows, block_index * key_block, key_block, 0
                )
                return single_block(inner_state, part_rows, block_index * key_block)

            return lax.fori_loop(0, row_count // key_block, sub_block, carry_state)
        return single_block(carry_state, block_rows, offset)

    return fold_keys


def on_device(tokens, projection, context_cotangent):
    score_scale = HEAD_DIMENSION ** (-0.5)
    local_rows = tokens.shape[0]
    rows_all = local_rows * QUERY_PER_GROUP
    first_row = lax.axis_index("seq") * local_rows
    query_pos = first_row + jnp.arange(rows_all, dtype=jnp.int32) // QUERY_PER_GROUP

    def split_heads(projected_weight):
        reshaped_grads = projected_weight.reshape(local_rows, QUERY_PER_GROUP + 2, HEAD_DIMENSION)
        query_rows = reshaped_grads[:, :QUERY_PER_GROUP].reshape(rows_all, HEAD_DIMENSION)
        key_value = reshaped_grads[:, QUERY_PER_GROUP:].reshape(local_rows, 2 * HEAD_DIMENSION)
        return (query_rows, key_value)

    def empty_state():
        return (
            jnp.full((rows_all,), masked_score, jnp.float32),
            jnp.zeros((rows_all,), jnp.float32),
            jnp.zeros((rows_all, HEAD_DIMENSION), jnp.float32),
        )

    projected_weight = jnp.dot(tokens, projection, preferred_element_type=jnp.float32).astype(
        jnp.bfloat16
    )
    query_rows, key_value = split_heads(projected_weight)
    gathered = lax.all_gather(key_value, "seq", axis=0, tiled=True)
    total_rows = gathered.shape[0]
    block_size = min(key_block, total_rows)
    needed = (first_row + local_rows - 1) // block_size + 1
    fold_first = attend_fold(query_rows, query_pos, score_scale)

    def forward_step(block_index, carry_state):
        block_rows = lax.dynamic_slice_in_dim(gathered, block_index * block_size, block_size, 0)
        return fold_first(carry_state, block_rows, block_index * block_size)

    running_max, row_total, context_sum = lax.fori_loop(0, needed, forward_step, empty_state())
    context = (context_sum / row_total[:, None]).astype(jnp.bfloat16)
    log_total = running_max + jnp.log(row_total)
    grad_rows = context_cotangent.reshape(rows_all, HEAD_DIMENSION)
    row_delta = jnp.sum(grad_rows.astype(jnp.float32) * context.astype(jnp.float32), axis=1)
    contract_rows = (((0,), (0,)), ((), ()))

    def backward_step(block_index, carry_state):
        query_grad, key_terms = carry_state
        offset = block_index * block_size
        block_rows = lax.dynamic_slice_in_dim(gathered, offset, block_size, 0)
        key_rows = block_rows[:, :HEAD_DIMENSION]
        value_rows = block_rows[:, HEAD_DIMENSION:]
        scores = jnp.dot(query_rows, key_rows.T, preferred_element_type=jnp.float32) * score_scale
        key_pos = offset + jnp.arange(block_size, dtype=jnp.int32)
        allowed = key_pos[None, :] <= query_pos[:, None]
        probs_full = jnp.where(allowed, jnp.exp(scores - log_total[:, None]), 0.0)
        probs_half = probs_full.astype(jnp.bfloat16)
        prob_grad = jnp.dot(grad_rows, value_rows.T, preferred_element_type=jnp.float32)
        score_grad = (probs_full * (prob_grad - row_delta[:, None]) * score_scale).astype(
            jnp.bfloat16
        )
        query_grad = query_grad + jnp.dot(score_grad, key_rows, preferred_element_type=jnp.float32)
        key_grad = lax.dot_general(
            score_grad, query_rows, contract_rows, preferred_element_type=jnp.float32
        )
        value_grad = lax.dot_general(
            probs_half, grad_rows, contract_rows, preferred_element_type=jnp.float32
        )
        key_terms = lax.dynamic_update_slice_in_dim(
            key_terms, jnp.concatenate([key_grad, value_grad], axis=1), offset, 0
        )
        return (query_grad, key_terms)

    initial = (
        jnp.zeros((rows_all, HEAD_DIMENSION), jnp.float32),
        jnp.zeros((total_rows, 2 * HEAD_DIMENSION), jnp.float32),
    )
    query_grad, key_terms = lax.fori_loop(0, needed, backward_step, initial)
    key_value_grad = lax.psum_scatter(key_terms, "seq", scatter_dimension=0, tiled=True).astype(
        jnp.bfloat16
    )
    head_grads = jnp.concatenate(
        [
            query_grad.astype(jnp.bfloat16).reshape(local_rows, QUERY_PER_GROUP * HEAD_DIMENSION),
            key_value_grad,
        ],
        axis=1,
    )
    grad_term = lax.dot_general(
        tokens, head_grads, contract_rows, preferred_element_type=jnp.float32
    )
    normalizing_scale = math.sqrt(
        INPUT_FEATURES * KEY_VALUE_HEADS * (QUERY_PER_GROUP + 2) * HEAD_DIMENSION
    )
    ascent_radius = 0.2 * math.sqrt(KEY_VALUE_HEADS * (QUERY_PER_GROUP + 2) * HEAD_DIMENSION)
    weight_grad = lax.psum(grad_term, "seq")
    square_sum = lax.psum(jnp.sum(weight_grad * weight_grad), "head")
    grad_norm = jnp.sqrt(square_sum)
    share_rows = INPUT_FEATURES // lax.axis_size("seq")
    own_grad = lax.dynamic_slice_in_dim(
        weight_grad, lax.axis_index("seq") * share_rows, share_rows, 0
    )
    direction = own_grad * (normalizing_scale / grad_norm)
    moved_weights = (
        projection.astype(jnp.float32) + ascent_radius / grad_norm * weight_grad
    ).astype(jnp.bfloat16)
    projected_new = jnp.dot(tokens, moved_weights, preferred_element_type=jnp.float32).astype(
        jnp.bfloat16
    )
    query_new, key_value_new = split_heads(projected_new)
    fold_new = attend_fold(query_new, query_pos, score_scale)
    final_state = fold_new(
        empty_state(), lax.all_gather(key_value_new, "seq", axis=0, tiled=True), jnp.int32(0)
    )
    perturbed = (
        (final_state[2] / final_state[1][:, None])
        .astype(jnp.bfloat16)
        .reshape(local_rows, QUERY_PER_GROUP * HEAD_DIMENSION)
    )
    return (perturbed, direction)


CONTRACT_LAST = (((1,), (1,)), ((), ()))
CONTRACT_FIRST = (((0,), (0,)), ((), ()))
SCALE = HEAD_DIMENSION ** (-0.5)
SCALE_LOG2 = SCALE * math.log2(math.e)
QW = QUERY_PER_GROUP * HEAD_DIMENSION
D = HEAD_DIMENSION
VMEM_BUDGET = 60 * 1024 * 1024


def flip(index, mask):
    bit = 1
    while bit <= mask:
        if mask & bit:
            index = index + bit - 2 * bit * ((index // bit) % 2)
        bit *= 2
    return index


def resident_kernel(
    seq_size, radius, root, tokens_ref, cotangent_ref, projection_hbm, out, direction,
    tokens, cotangent, projection, projected, base_q, base_kv, key_t, grads,
    key_sum, value_sum, weight_half, own_grad, move_q, move_kv, norms,
    local_sem, load_sem, own_sent, own_sent_c, line_sent, line_sent_c, fold_sent, fold_sent_c,
    got, got_c, across_sent, pair_sent, relay_sent, across_got, pair_got, relay_got,
    norm_sent, norm_got,
):
    s = lax.axis_index("seq")
    h = lax.axis_index("head")
    local_rows = tokens_ref.shape[0]
    parts, total, width = tokens.shape
    tile = min(256, total)
    share = own_grad.shape[0]

    def rows_of(index):
        return pl.ds(pl.multiple_of(index * local_rows, local_rows), local_rows)

    def columns_of(index):
        return pl.ds(pl.multiple_of(index * width, width), width)

    mesh_type = pl.DeviceIdType.MESH
    partner = flip(s, 1)
    side = s % 2
    place_on_line = s // 2
    length_of_line = seq_size // 2
    has_right = place_on_line < length_of_line - 1
    has_left = place_on_line > 0

    def remote(source, target, send, receive, to_s, to_h):
        return pltpu.make_async_remote_copy(
            src_ref=source, dst_ref=target, send_sem=send, recv_sem=receive,
            device_id=(to_s, to_h), device_id_type=mesh_type,
        )

    def line_block(j):
        near = jnp.minimum(place_on_line, length_of_line - 1 - place_on_line)
        alternate = place_on_line - 1 - j // 2 if j % 2 == 0 else place_on_line + 1 + j // 2
        beyond = jnp.where(place_on_line > near, length_of_line - 2 - j, j + 1)
        return jnp.where(j < 2 * near, alternate, beyond)

    load = pltpu.make_async_copy(projection_hbm, projection, load_sem)
    load.start()
    barrier = pltpu.get_barrier_semaphore()

    def greet(to_s, to_h):
        pl.semaphore_signal(barrier, inc=1, device_id=(to_s, to_h), device_id_type=mesh_type)

    greet(partner, h)
    for q in range(1, parts):
        greet(s, flip(h, q))

    @pl.when(has_right)
    def _():
        greet(s + 2, h)

    @pl.when(has_left)
    def _():
        greet(s - 2, h)

    both_sides = jnp.minimum(place_on_line, 1) + jnp.minimum(length_of_line - 1 - place_on_line, 1)
    pl.semaphore_wait(barrier, parts + both_sides)

    sent = []

    def send(source, target, send_sem, receive, to_s, to_h, when=None):
        copy = remote(source, target, send_sem, receive, to_s, to_h)
        sent.append((copy, when))
        if when is None:
            copy.start()
        else:

            @pl.when(when)
            def _():
                copy.start()

    own_rows = rows_of(s)

    own_tokens = (tokens_ref.at[:, columns_of(h)], tokens.at[h, own_rows])
    own_cotangent = (cotangent_ref, cotangent.at[own_rows])

    def send_line(source, place, send_sem, receive):
        send(source, place, send_sem.at[0], receive.at[s], s + 2, h, has_right)
        send(source, place, send_sem.at[1], receive.at[s], s - 2, h, has_left)

    send_line(*own_tokens, own_sent, got)
    send(*own_tokens, own_sent.at[2], got.at[s], partner, h)
    send(*own_cotangent, own_sent_c.at[2], got_c.at[s], partner, h)
    local = [pltpu.make_async_copy(tokens_ref.at[:, columns_of(q)], tokens.at[q, own_rows],
                                   local_sem.at[q]) for q in range(parts)]
    local.append(pltpu.make_async_copy(cotangent_ref, cotangent.at[own_rows],
                                       local_sem.at[parts]))
    for copy in local:
        copy.start()

    def token_rows(rows, weights, columns):
        acc = jnp.dot(tokens[0, rows, :], weights[pl.ds(0, width), columns],
                      preferred_element_type=jnp.float32)
        for q in range(1, parts):
            acc += jnp.dot(tokens[q, rows, :], weights[pl.ds(q * width, width), columns],
                           preferred_element_type=jnp.float32)
        return acc

    def index_of(kind, j):
        if kind == "own":
            return s
        if kind == "pair":
            return partner
        return line_block(j) * 2 + (side if kind == "line" else 1 - side)

    def wait_for(place, semaphore):
        remote(place, place, own_sent.at[2], semaphore, partner, h).wait_recv()

    def project(kind, j=0):
        index = index_of(kind, j)
        rows = rows_of(index)
        if kind != "own":
            wait_for(tokens.at[flip(h, 1), rows], pair_got.at[index])
            wait_for(tokens.at[flip(h, 3), rows], relay_got.at[index])
        acc = token_rows(rows, projection, slice(None))
        if kind == "own":
            base_q[...] = acc[:, :QW]
        base_kv[rows, :] = acc[:, QW:]
        half = acc.astype(jnp.bfloat16)
        projected[rows, :] = half
        half_f = half.astype(jnp.float32)
        key_t[:, rows] = half_f[:, QW : QW + D].T.astype(jnp.bfloat16)

    def pass_on(place, index, line, fold, receive):
        ahead = index // 2 < place_on_line
        to_s = jnp.where(ahead, s + 2, s - 2)
        more = jnp.where(ahead, place_on_line < length_of_line - 1, place_on_line > 0)
        send(place, place, line.at[index], receive.at[index], to_s, h, more)
        send(place, place, fold.at[index], receive.at[index], partner, h)

    def arrived(kind, j=0):
        index = index_of(kind, j)
        place = tokens.at[h, rows_of(index)]
        wait_for(place, got.at[index])
        if kind == "line":
            pass_on(place, index, line_sent, fold_sent, got)
        send(place, place, across_sent.at[index], across_got.at[index], s, flip(h, 2))
        send(place, place, pair_sent.at[index], pair_got.at[index], s, flip(h, 1))

    def arrived_c(kind, j=0):
        index = index_of(kind, j)
        place = cotangent.at[rows_of(index)]
        wait_for(place, got_c.at[index])
        if kind == "line":
            pass_on(place, index, line_sent_c, fold_sent_c, got_c)

    def relay(kind, j=0):
        index = index_of(kind, j)
        place = tokens.at[flip(h, 2), rows_of(index)]
        wait_for(place, across_got.at[index])
        send(place, place, relay_sent.at[index], relay_got.at[index], s, flip(h, 1))

    for copy in local:
        copy.wait()

    steps = length_of_line - 1
    order = [("line", 0), ("pair", 0)]
    for j in range(1, steps):
        order += [("line", j), ("fold", j - 1)]
    order.append(("fold", steps - 1))
    queue = [("own", 0)] + order
    cotangents = [("line", j) for j in range(steps)]
    for position, item in enumerate(order):
        arrived(*item)
        if item == ("line", 0):
            send_line(*own_cotangent, own_sent_c, got_c)
        if position == 3:
            load.wait()
        if position >= 3:
            relay(*order[position - 3])
            project(*queue.pop(0))
        if position >= 4 and position % 2 == 0 and cotangents:
            arrived_c(*cotangents.pop(0))
    for item in order[-3:]:
        if cotangents:
            arrived_c(*cotangents.pop(0))
        relay(*item)
        project(*queue.pop(0))
    while cotangents:
        arrived_c(*cotangents.pop(0))
    while queue:
        project(*queue.pop(0))
    arrived_c("pair")
    for j in range(steps):
        arrived_c("fold", j)

    key_sum[...] = jnp.zeros_like(key_sum)
    value_sum[...] = jnp.zeros_like(value_sum)

    allowed = lax.broadcasted_iota(jnp.int32, (tile, tile), 0) <= lax.broadcasted_iota(
        jnp.int32, (tile, tile), 1
    )
    for block in range(total // tile):
        length = (block + 1) * tile
        rows = slice(block * tile, length)

        @pl.loop(0, QUERY_PER_GROUP, unroll=2)
        def _(head):
            columns = pl.ds(pl.multiple_of(head * D, D), D)
            query = projected[rows, columns]
            out_grad = cotangent[rows, columns]
            scores = lax.dot_general(projected[:length, QW : QW + D], query, CONTRACT_LAST,
                                     preferred_element_type=jnp.float32)
            last = jnp.where(allowed, scores[block * tile :], masked_score)
            scores = last if block == 0 else jnp.concatenate([scores[: block * tile], last], 0)
            top = jnp.max(scores, axis=0, keepdims=True)
            weights = jnp.exp2(scores * SCALE_LOG2 - top * SCALE_LOG2)
            probs = weights * (1.0 / jnp.sum(weights, axis=0, keepdims=True))
            probs_half = probs.astype(jnp.bfloat16)
            prob_grad = lax.dot_general(projected[:length, QW + D :], out_grad, CONTRACT_LAST,
                                        preferred_element_type=jnp.float32)
            weighted = probs * prob_grad
            delta = jnp.sum(weighted, axis=0, keepdims=True)
            score_grad = (weighted - probs * delta).astype(jnp.bfloat16)
            query_t = jnp.dot(key_t[:, :length], score_grad, preferred_element_type=jnp.float32)
            grads[rows, columns] = (query_t * SCALE).T.astype(jnp.bfloat16)
            key_sum[:length, :] += jnp.dot(score_grad, query, preferred_element_type=jnp.float32)
            value_sum[:length, :] += jnp.dot(probs_half, out_grad,
                                             preferred_element_type=jnp.float32)

    grads[:, QW : QW + D] = (key_sum[...] * SCALE).astype(jnp.bfloat16)
    grads[:, QW + D :] = value_sum[...].astype(jnp.bfloat16)

    per_part = width // share
    norms[0] = jnp.zeros_like(norms[0])

    @pl.loop(0, parts * per_part)
    def _(chunk):
        columns = pl.ds(pl.multiple_of((chunk % per_part) * share, share), share)
        rows = pl.ds(pl.multiple_of(chunk * share, share), share)
        block = lax.dot_general(tokens[chunk // per_part, :, columns], grads[...], CONTRACT_FIRST,
                                preferred_element_type=jnp.float32)
        squared = block * block
        lanes = squared[:, :128]
        for start in range(128, squared.shape[1], 128):
            lanes += squared[:, start : start + 128]
        norms[0] += jnp.sum(lanes.reshape(share // 8, 8, 128), axis=0)
        weight_half[rows, :] = block.astype(jnp.bfloat16)

        @pl.when(chunk == s)
        def _():
            own_grad[...] = block

    move_q[...] = token_rows(own_rows, weight_half, slice(0, QW))
    for q in range(1, parts):
        send(norms.at[0], norms.at[q], norm_sent.at[q], norm_got.at[q], s, flip(h, q))

    @pl.loop(0, total // tile)
    def _(block):
        rows = pl.ds(pl.multiple_of(block * tile, tile), tile)
        move_kv[rows, :] = token_rows(rows, weight_half, slice(QW, None))

    for q in range(1, parts):
        remote(norms.at[q], norms.at[q], norm_sent.at[0], norm_got.at[q], s, flip(h, q)).wait_recv()
    square_sum = jnp.sum(jnp.sum(norms[...], axis=0), keepdims=True)
    inverse = 1.0 / jnp.sqrt(square_sum)
    direction[...] = own_grad[...] * (root * inverse)
    step_size = radius * inverse
    query = (base_q[...] + step_size * move_q[...]).astype(jnp.bfloat16)
    key_value = (base_kv[...] + step_size * move_kv[...]).astype(jnp.bfloat16)
    new_value_t = key_value[:, D:].astype(jnp.float32).T.astype(jnp.bfloat16)
    stacked = jnp.concatenate(
        [query[:, g * D : (g + 1) * D] for g in range(QUERY_PER_GROUP)], axis=0
    )
    scores = lax.dot_general(key_value[:, :D], stacked, CONTRACT_LAST,
                             preferred_element_type=jnp.float32)
    key_pos = lax.broadcasted_iota(jnp.int32, (total, local_rows), 0)
    row_pos = lax.broadcasted_iota(jnp.int32, (total, local_rows), 1) + s * local_rows
    visible = key_pos <= row_pos
    for g in range(QUERY_PER_GROUP):
        part = jnp.where(visible, scores[:, g * local_rows : (g + 1) * local_rows], masked_score)
        top = jnp.max(part, axis=0, keepdims=True)
        weights = jnp.exp2(part * SCALE_LOG2 - top * SCALE_LOG2)
        sums = jnp.sum(weights, axis=0, keepdims=True)
        context_t = jnp.dot(new_value_t, weights.astype(jnp.bfloat16),
                            preferred_element_type=jnp.float32) / sums
        out[:, g * D : (g + 1) * D] = context_t.T.astype(jnp.bfloat16)
    for copy, when in sent:
        if when is None:
            copy.wait_send()
        else:

            @pl.when(when)
            def _():
                copy.wait_send()


def resident_step(tokens, projection, cotangent):
    seq_size, parts = lax.axis_size("seq"), lax.axis_size("head")
    local_rows, features = tokens.shape
    columns = projection.shape[1]
    share = features // seq_size
    total = local_rows * seq_size
    f32, bf16 = jnp.float32, jnp.bfloat16
    root = math.sqrt(features * parts * columns)
    radius = 0.2 * math.sqrt(parts * columns)
    in_vmem = pl.BlockSpec(memory_space=pltpu.VMEM)
    return pl.pallas_call(
        functools.partial(resident_kernel, seq_size, radius, root),
        out_shape=(
            jax.ShapeDtypeStruct((local_rows, QW), bf16),
            jax.ShapeDtypeStruct((share, columns), f32),
        ),
        in_specs=[in_vmem, in_vmem, pl.BlockSpec(memory_space=pl.ANY)],
        out_specs=(in_vmem, in_vmem),
        scratch_shapes=[
            pltpu.VMEM((parts, total, features // parts), bf16),
            pltpu.VMEM((total, QW), bf16),
            pltpu.VMEM((features, columns), bf16),
            pltpu.VMEM((total, columns), bf16),
            pltpu.VMEM((local_rows, QW), f32),
            pltpu.VMEM((total, 2 * D), f32),
            pltpu.VMEM((D, total), bf16),
            pltpu.VMEM((total, columns), bf16),
            pltpu.VMEM((total, D), f32),
            pltpu.VMEM((total, D), f32),
            pltpu.VMEM((features, columns), bf16),
            pltpu.VMEM((share, columns), f32),
            pltpu.VMEM((local_rows, QW), f32),
            pltpu.VMEM((total, 2 * D), f32),
            pltpu.VMEM((parts, 8, 128), f32),
            pltpu.SemaphoreType.DMA((parts + 1,)),
            pltpu.SemaphoreType.DMA,
        ]
        + [pltpu.SemaphoreType.DMA((seq_size,))] * 14
        + [pltpu.SemaphoreType.DMA((parts,))] * 2,
        compiler_params=pltpu.CompilerParams(
            collective_id=0, has_side_effects=True, vmem_limit_bytes=VMEM_BUDGET
        ),
        name="resident",
    )(tokens, cotangent, projection)


def fits(local_rows, features, columns, seq_size, head_size):
    total = local_rows * seq_size
    share = features // seq_size
    held = total * (2 * features + 2 * QW + 12 * columns + 24 * D) + 4 * features * columns
    pairs = seq_size >= 8 and seq_size & (seq_size - 1) == 0 and head_size == 4
    aligned = share % 128 == 0 and (features // head_size) % share == 0 and local_rows % 128 == 0
    return pairs and aligned and held < VMEM_BUDGET // 2


def step(tokens, projection, context_cotangent):
    sizes = (*tokens.shape, projection.shape[1], lax.axis_size("seq"), lax.axis_size("head"))
    if fits(*sizes):
        return resident_step(tokens, projection, context_cotangent)
    return on_device(tokens, projection, context_cotangent)


def solution(mesh):
    return jax.shard_map(
        step,
        mesh=mesh,
        in_specs=(P("seq", None), P(None, "head"), P("seq", "head")),
        out_specs=(P("seq", "head"), P("seq", "head")),
        check_vma=False,
    )
```

```python
import functools
import math

import jax
import jax.numpy as jnp
from jax import lax
from jax.experimental import pallas as pl
from jax.experimental.pallas import tpu as pltpu
from jax.sharding import PartitionSpec as P

INPUT_FEATURES = 2048
KEY_VALUE_HEADS = 4
HEAD_DIMENSION = 128
QUERY_PER_GROUP = 4


masked_score = -1e30
key_block = 512


def attend_fold(query_rows, query_pos, score_scale):
    head_size = query_rows.shape[1]

    def single_block(carry_state, block_rows, offset):
        running_max, row_total, context_sum = carry_state
        key_rows = block_rows[:, :head_size]
        value_rows = block_rows[:, head_size:].astype(jnp.float32)
        scores = jnp.dot(query_rows, key_rows.T, preferred_element_type=jnp.float32) * score_scale
        key_pos = offset + jnp.arange(block_rows.shape[0], dtype=jnp.int32)
        allowed = key_pos[None, :] <= query_pos[:, None]
        scores = jnp.where(allowed, scores, masked_score)
        new_max = jnp.maximum(running_max, jnp.max(scores, axis=1))
        factor = jnp.exp(running_max - new_max)
        weights = jnp.where(allowed, jnp.exp(scores - new_max[:, None]), 0.0)
        row_total = row_total * factor + jnp.sum(weights, axis=1)
        context_sum = context_sum * factor[:, None] + jnp.dot(
            weights, value_rows, precision=lax.Precision.HIGHEST, preferred_element_type=jnp.float32
        )
        return (new_max, row_total, context_sum)

    def fold_keys(carry_state, block_rows, offset):
        row_count = block_rows.shape[0]
        if row_count > key_block and row_count % key_block == 0:

            def sub_block(block_index, inner_state):
                part_rows = lax.dynamic_slice_in_dim(
                    block_rows, block_index * key_block, key_block, 0
                )
                return single_block(inner_state, part_rows, block_index * key_block)

            return lax.fori_loop(0, row_count // key_block, sub_block, carry_state)
        return single_block(carry_state, block_rows, offset)

    return fold_keys


def on_device(tokens, projection, context_cotangent):
    score_scale = HEAD_DIMENSION ** (-0.5)
    local_rows = tokens.shape[0]
    rows_all = local_rows * QUERY_PER_GROUP
    first_row = lax.axis_index("seq") * local_rows
    query_pos = first_row + jnp.arange(rows_all, dtype=jnp.int32) // QUERY_PER_GROUP

    def split_heads(projected_weight):
        reshaped_grads = projected_weight.reshape(local_rows, QUERY_PER_GROUP + 2, HEAD_DIMENSION)
        query_rows = reshaped_grads[:, :QUERY_PER_GROUP].reshape(rows_all, HEAD_DIMENSION)
        key_value = reshaped_grads[:, QUERY_PER_GROUP:].reshape(local_rows, 2 * HEAD_DIMENSION)
        return (query_rows, key_value)

    def empty_state():
        return (
            jnp.full((rows_all,), masked_score, jnp.float32),
            jnp.zeros((rows_all,), jnp.float32),
            jnp.zeros((rows_all, HEAD_DIMENSION), jnp.float32),
        )

    projected_weight = jnp.dot(tokens, projection, preferred_element_type=jnp.float32).astype(
        jnp.bfloat16
    )
    query_rows, key_value = split_heads(projected_weight)
    gathered = lax.all_gather(key_value, "seq", axis=0, tiled=True)
    total_rows = gathered.shape[0]
    block_size = min(key_block, total_rows)
    needed = (first_row + local_rows - 1) // block_size + 1
    fold_first = attend_fold(query_rows, query_pos, score_scale)

    def forward_step(block_index, carry_state):
        block_rows = lax.dynamic_slice_in_dim(gathered, block_index * block_size, block_size, 0)
        return fold_first(carry_state, block_rows, block_index * block_size)

    running_max, row_total, context_sum = lax.fori_loop(0, needed, forward_step, empty_state())
    context = (context_sum / row_total[:, None]).astype(jnp.bfloat16)
    log_total = running_max + jnp.log(row_total)
    grad_rows = context_cotangent.reshape(rows_all, HEAD_DIMENSION)
    row_delta = jnp.sum(grad_rows.astype(jnp.float32) * context.astype(jnp.float32), axis=1)
    contract_rows = (((0,), (0,)), ((), ()))

    def backward_step(block_index, carry_state):
        query_grad, key_terms = carry_state
        offset = block_index * block_size
        block_rows = lax.dynamic_slice_in_dim(gathered, offset, block_size, 0)
        key_rows = block_rows[:, :HEAD_DIMENSION]
        value_rows = block_rows[:, HEAD_DIMENSION:]
        scores = jnp.dot(query_rows, key_rows.T, preferred_element_type=jnp.float32) * score_scale
        key_pos = offset + jnp.arange(block_size, dtype=jnp.int32)
        allowed = key_pos[None, :] <= query_pos[:, None]
        probs_full = jnp.where(allowed, jnp.exp(scores - log_total[:, None]), 0.0)
        probs_half = probs_full.astype(jnp.bfloat16)
        prob_grad = jnp.dot(grad_rows, value_rows.T, preferred_element_type=jnp.float32)
        score_grad = (probs_full * (prob_grad - row_delta[:, None]) * score_scale).astype(
            jnp.bfloat16
        )
        query_grad = query_grad + jnp.dot(score_grad, key_rows, preferred_element_type=jnp.float32)
        key_grad = lax.dot_general(
            score_grad, query_rows, contract_rows, preferred_element_type=jnp.float32
        )
        value_grad = lax.dot_general(
            probs_half, grad_rows, contract_rows, preferred_element_type=jnp.float32
        )
        key_terms = lax.dynamic_update_slice_in_dim(
            key_terms, jnp.concatenate([key_grad, value_grad], axis=1), offset, 0
        )
        return (query_grad, key_terms)

    initial = (
        jnp.zeros((rows_all, HEAD_DIMENSION), jnp.float32),
        jnp.zeros((total_rows, 2 * HEAD_DIMENSION), jnp.float32),
    )
    query_grad, key_terms = lax.fori_loop(0, needed, backward_step, initial)
    key_value_grad = lax.psum_scatter(key_terms, "seq", scatter_dimension=0, tiled=True).astype(
        jnp.bfloat16
    )
    head_grads = jnp.concatenate(
        [
            query_grad.astype(jnp.bfloat16).reshape(local_rows, QUERY_PER_GROUP * HEAD_DIMENSION),
            key_value_grad,
        ],
        axis=1,
    )
    grad_term = lax.dot_general(
        tokens, head_grads, contract_rows, preferred_element_type=jnp.float32
    )
    normalizing_scale = math.sqrt(
        INPUT_FEATURES * KEY_VALUE_HEADS * (QUERY_PER_GROUP + 2) * HEAD_DIMENSION
    )
    ascent_radius = 0.2 * math.sqrt(KEY_VALUE_HEADS * (QUERY_PER_GROUP + 2) * HEAD_DIMENSION)
    weight_grad = lax.psum(grad_term, "seq")
    square_sum = lax.psum(jnp.sum(weight_grad * weight_grad), "head")
    grad_norm = jnp.sqrt(square_sum)
    share_rows = INPUT_FEATURES // lax.axis_size("seq")
    own_grad = lax.dynamic_slice_in_dim(
        weight_grad, lax.axis_index("seq") * share_rows, share_rows, 0
    )
    direction = own_grad * (normalizing_scale / grad_norm)
    moved_weights = (
        projection.astype(jnp.float32) + ascent_radius / grad_norm * weight_grad
    ).astype(jnp.bfloat16)
    projected_new = jnp.dot(tokens, moved_weights, preferred_element_type=jnp.float32).astype(
        jnp.bfloat16
    )
    query_new, key_value_new = split_heads(projected_new)
    fold_new = attend_fold(query_new, query_pos, score_scale)
    final_state = fold_new(
        empty_state(), lax.all_gather(key_value_new, "seq", axis=0, tiled=True), jnp.int32(0)
    )
    perturbed = (
        (final_state[2] / final_state[1][:, None])
        .astype(jnp.bfloat16)
        .reshape(local_rows, QUERY_PER_GROUP * HEAD_DIMENSION)
    )
    return (perturbed, direction)


CONTRACT_LAST = (((1,), (1,)), ((), ()))
CONTRACT_FIRST = (((0,), (0,)), ((), ()))
SCALE = HEAD_DIMENSION ** (-0.5)
SCALE_LOG2 = SCALE * math.log2(math.e)
QW = QUERY_PER_GROUP * HEAD_DIMENSION
D = HEAD_DIMENSION
VMEM_BUDGET = 60 * 1024 * 1024


def flip(index, mask):
    bit = 1
    while bit <= mask:
        if mask & bit:
            index = index + bit - 2 * bit * ((index // bit) % 2)
        bit *= 2
    return index


def resident_kernel(
    seq_size, radius, root, tokens_ref, cotangent_ref, projection_hbm, out, direction,
    tokens, cotangent, projection, projected, base_q, base_kv, key_t, grads,
    key_sum, value_sum, weight_half, own_grad, move_q, move_kv, norms,
    local_sem, load_sem, own_sent, own_sent_c, line_sent, line_sent_c, fold_sent, fold_sent_c,
    got, got_c, across_sent, pair_sent, relay_sent, across_got, pair_got, relay_got,
    norm_sent, norm_got,
):
    s = lax.axis_index("seq")
    h = lax.axis_index("head")
    local_rows = tokens_ref.shape[0]
    parts, total, width = tokens.shape
    tile = min(256, total)
    share = own_grad.shape[0]

    def rows_of(index):
        return pl.ds(pl.multiple_of(index * local_rows, local_rows), local_rows)

    def columns_of(index):
        return pl.ds(pl.multiple_of(index * width, width), width)

    mesh_type = pl.DeviceIdType.MESH
    partner = flip(s, 1)
    side = s % 2
    place_on_line = s // 2
    length_of_line = seq_size // 2
    has_right = place_on_line < length_of_line - 1
    has_left = place_on_line > 0

    def remote(source, target, send, receive, to_s, to_h):
        return pltpu.make_async_remote_copy(
            src_ref=source, dst_ref=target, send_sem=send, recv_sem=receive,
            device_id=(to_s, to_h), device_id_type=mesh_type,
        )

    def line_block(j):
        near = jnp.minimum(place_on_line, length_of_line - 1 - place_on_line)
        alternate = place_on_line - 1 - j // 2 if j % 2 == 0 else place_on_line + 1 + j // 2
        beyond = jnp.where(place_on_line > near, length_of_line - 2 - j, j + 1)
        return jnp.where(j < 2 * near, alternate, beyond)

    load = pltpu.make_async_copy(projection_hbm, projection, load_sem)
    load.start()
    barrier = pltpu.get_barrier_semaphore()

    def greet(to_s, to_h):
        pl.semaphore_signal(barrier, inc=1, device_id=(to_s, to_h), device_id_type=mesh_type)

    greet(partner, h)
    for q in range(1, parts):
        greet(s, flip(h, q))

    @pl.when(has_right)
    def _():
        greet(s + 2, h)

    @pl.when(has_left)
    def _():
        greet(s - 2, h)

    both_sides = jnp.minimum(place_on_line, 1) + jnp.minimum(length_of_line - 1 - place_on_line, 1)
    pl.semaphore_wait(barrier, parts + both_sides)

    sent = []

    def send(source, target, send_sem, receive, to_s, to_h, when=None):
        copy = remote(source, target, send_sem, receive, to_s, to_h)
        sent.append((copy, when))
        if when is None:
            copy.start()
        else:

            @pl.when(when)
            def _():
                copy.start()

    own_rows = rows_of(s)

    own_tokens = (tokens_ref.at[:, columns_of(h)], tokens.at[h, own_rows])
    own_cotangent = (cotangent_ref, cotangent.at[own_rows])

    def send_line(source, place, send_sem, receive):
        send(source, place, send_sem.at[0], receive.at[s], s + 2, h, has_right)
        send(source, place, send_sem.at[1], receive.at[s], s - 2, h, has_left)

    send_line(*own_tokens, own_sent, got)
    send(*own_tokens, own_sent.at[2], got.at[s], partner, h)
    send(*own_cotangent, own_sent_c.at[2], got_c.at[s], partner, h)
    local = [pltpu.make_async_copy(tokens_ref.at[:, columns_of(q)], tokens.at[q, own_rows],
                                   local_sem.at[q]) for q in range(parts)]
    local.append(pltpu.make_async_copy(cotangent_ref, cotangent.at[own_rows],
                                       local_sem.at[parts]))
    for copy in local:
        copy.start()

    def token_rows(rows, weights, columns):
        acc = jnp.dot(tokens[0, rows, :], weights[pl.ds(0, width), columns],
                      preferred_element_type=jnp.float32)
        for q in range(1, parts):
            acc += jnp.dot(tokens[q, rows, :], weights[pl.ds(q * width, width), columns],
                           preferred_element_type=jnp.float32)
        return acc

    def index_of(kind, j):
        if kind == "own":
            return s
        if kind == "pair":
            return partner
        return line_block(j) * 2 + (side if kind == "line" else 1 - side)

    def wait_for(place, semaphore):
        remote(place, place, own_sent.at[2], semaphore, partner, h).wait_recv()

    def project(kind, j=0):
        index = index_of(kind, j)
        rows = rows_of(index)
        if kind != "own":
            wait_for(tokens.at[flip(h, 1), rows], pair_got.at[index])
            wait_for(tokens.at[flip(h, 3), rows], relay_got.at[index])
        acc = token_rows(rows, projection, slice(None))
        if kind == "own":
            base_q[...] = acc[:, :QW]
        base_kv[rows, :] = acc[:, QW:]
        half = acc.astype(jnp.bfloat16)
        projected[rows, :] = half
        half_f = half.astype(jnp.float32)
        key_t[:, rows] = half_f[:, QW : QW + D].T.astype(jnp.bfloat16)

    def pass_on(place, index, line, fold, receive):
        ahead = index // 2 < place_on_line
        to_s = jnp.where(ahead, s + 2, s - 2)
        more = jnp.where(ahead, place_on_line < length_of_line - 1, place_on_line > 0)
        send(place, place, line.at[index], receive.at[index], to_s, h, more)
        send(place, place, fold.at[index], receive.at[index], partner, h)

    def arrived(kind, j=0):
        index = index_of(kind, j)
        place = tokens.at[h, rows_of(index)]
        wait_for(place, got.at[index])
        if kind == "line":
            pass_on(place, index, line_sent, fold_sent, got)
        send(place, place, across_sent.at[index], across_got.at[index], s, flip(h, 2))
        send(place, place, pair_sent.at[index], pair_got.at[index], s, flip(h, 1))

    def arrived_c(kind, j=0):
        index = index_of(kind, j)
        place = cotangent.at[rows_of(index)]
        wait_for(place, got_c.at[index])
        if kind == "line":
            pass_on(place, index, line_sent_c, fold_sent_c, got_c)

    def relay(kind, j=0):
        index = index_of(kind, j)
        place = tokens.at[flip(h, 2), rows_of(index)]
        wait_for(place, across_got.at[index])
        send(place, place, relay_sent.at[index], relay_got.at[index], s, flip(h, 1))

    for copy in local:
        copy.wait()

    steps = length_of_line - 1
    order = [("line", 0), ("pair", 0)]
    for j in range(1, steps):
        order += [("line", j), ("fold", j - 1)]
    order.append(("fold", steps - 1))
    queue = [("own", 0)] + order
    cotangents = [("line", j) for j in range(steps)]
    for position, item in enumerate(order):
        arrived(*item)
        if item == ("line", 0):
            send_line(*own_cotangent, own_sent_c, got_c)
        if position == 3:
            load.wait()
        if position >= 3:
            relay(*order[position - 3])
            project(*queue.pop(0))
        if position >= 4 and position % 2 == 0 and cotangents:
            arrived_c(*cotangents.pop(0))
    for item in order[-3:]:
        if cotangents:
            arrived_c(*cotangents.pop(0))
        relay(*item)
        project(*queue.pop(0))
    while cotangents:
        arrived_c(*cotangents.pop(0))
    while queue:
        project(*queue.pop(0))
    arrived_c("pair")
    for j in range(steps):
        arrived_c("fold", j)

    key_sum[...] = jnp.zeros_like(key_sum)
    value_sum[...] = jnp.zeros_like(value_sum)

    allowed = lax.broadcasted_iota(jnp.int32, (tile, tile), 0) <= lax.broadcasted_iota(
        jnp.int32, (tile, tile), 1
    )
    for block in range(total // tile):
        length = (block + 1) * tile
        rows = slice(block * tile, length)

        @pl.loop(0, QUERY_PER_GROUP, unroll=4)
        def _(head):
            columns = pl.ds(pl.multiple_of(head * D, D), D)
            query = projected[rows, columns]
            out_grad = cotangent[rows, columns]
            scores = lax.dot_general(projected[:length, QW : QW + D], query, CONTRACT_LAST,
                                     preferred_element_type=jnp.float32)
            last = jnp.where(allowed, scores[block * tile :], masked_score)
            scores = last if block == 0 else jnp.concatenate([scores[: block * tile], last], 0)
            top = jnp.max(scores, axis=0, keepdims=True)
            weights = jnp.exp2(scores * SCALE_LOG2 - top * SCALE_LOG2)
            probs = weights * (1.0 / jnp.sum(weights, axis=0, keepdims=True))
            probs_half = probs.astype(jnp.bfloat16)
            prob_grad = lax.dot_general(projected[:length, QW + D :], out_grad, CONTRACT_LAST,
                                        preferred_element_type=jnp.float32)
            weighted = probs * prob_grad
            delta = jnp.sum(weighted, axis=0, keepdims=True)
            score_grad = (weighted - probs * delta).astype(jnp.bfloat16)
            query_t = jnp.dot(key_t[:, :length], score_grad, preferred_element_type=jnp.float32)
            grads[rows, columns] = (query_t * SCALE).T.astype(jnp.bfloat16)
            key_sum[:length, :] += jnp.dot(score_grad, query, preferred_element_type=jnp.float32)
            value_sum[:length, :] += jnp.dot(probs_half, out_grad,
                                             preferred_element_type=jnp.float32)

    grads[:, QW : QW + D] = (key_sum[...] * SCALE).astype(jnp.bfloat16)
    grads[:, QW + D :] = value_sum[...].astype(jnp.bfloat16)

    per_part = width // share
    norms[0] = jnp.zeros_like(norms[0])

    @pl.loop(0, parts * per_part, unroll=2)
    def _(chunk):
        columns = pl.ds(pl.multiple_of((chunk % per_part) * share, share), share)
        rows = pl.ds(pl.multiple_of(chunk * share, share), share)
        block = lax.dot_general(tokens[chunk // per_part, :, columns], grads[...], CONTRACT_FIRST,
                                preferred_element_type=jnp.float32)
        squared = block * block
        lanes = squared[:, :128]
        for start in range(128, squared.shape[1], 128):
            lanes += squared[:, start : start + 128]
        norms[0] += jnp.sum(lanes.reshape(share // 8, 8, 128), axis=0)
        weight_half[rows, :] = block.astype(jnp.bfloat16)

        @pl.when(chunk == s)
        def _():
            own_grad[...] = block

    move_q[...] = token_rows(own_rows, weight_half, slice(0, QW))
    for q in range(1, parts):
        send(norms.at[0], norms.at[q], norm_sent.at[q], norm_got.at[q], s, flip(h, q))

    @pl.loop(0, total // tile)
    def _(block):
        rows = pl.ds(pl.multiple_of(block * tile, tile), tile)
        move_kv[rows, :] = token_rows(rows, weight_half, slice(QW, None))

    for q in range(1, parts):
        remote(norms.at[q], norms.at[q], norm_sent.at[0], norm_got.at[q], s, flip(h, q)).wait_recv()
    square_sum = jnp.sum(jnp.sum(norms[...], axis=0), keepdims=True)
    inverse = 1.0 / jnp.sqrt(square_sum)
    direction[...] = own_grad[...] * (root * inverse)
    step_size = radius * inverse
    query = (base_q[...] + step_size * move_q[...]).astype(jnp.bfloat16)
    key_value = (base_kv[...] + step_size * move_kv[...]).astype(jnp.bfloat16)
    new_value_t = key_value[:, D:].astype(jnp.float32).T.astype(jnp.bfloat16)
    stacked = jnp.concatenate(
        [query[:, g * D : (g + 1) * D] for g in range(QUERY_PER_GROUP)], axis=0
    )
    scores = lax.dot_general(key_value[:, :D], stacked, CONTRACT_LAST,
                             preferred_element_type=jnp.float32)
    key_pos = lax.broadcasted_iota(jnp.int32, (total, local_rows), 0)
    row_pos = lax.broadcasted_iota(jnp.int32, (total, local_rows), 1) + s * local_rows
    visible = key_pos <= row_pos
    for g in range(QUERY_PER_GROUP):
        part = jnp.where(visible, scores[:, g * local_rows : (g + 1) * local_rows], masked_score)
        top = jnp.max(part, axis=0, keepdims=True)
        weights = jnp.exp2(part * SCALE_LOG2 - top * SCALE_LOG2)
        sums = jnp.sum(weights, axis=0, keepdims=True)
        context_t = jnp.dot(new_value_t, weights.astype(jnp.bfloat16),
                            preferred_element_type=jnp.float32) / sums
        out[:, g * D : (g + 1) * D] = context_t.T.astype(jnp.bfloat16)
    for copy, when in sent:
        if when is None:
            copy.wait_send()
        else:

            @pl.when(when)
            def _():
                copy.wait_send()


def resident_step(tokens, projection, cotangent):
    seq_size, parts = lax.axis_size("seq"), lax.axis_size("head")
    local_rows, features = tokens.shape
    columns = projection.shape[1]
    share = features // seq_size
    total = local_rows * seq_size
    f32, bf16 = jnp.float32, jnp.bfloat16
    root = math.sqrt(features * parts * columns)
    radius = 0.2 * math.sqrt(parts * columns)
    in_vmem = pl.BlockSpec(memory_space=pltpu.VMEM)
    return pl.pallas_call(
        functools.partial(resident_kernel, seq_size, radius, root),
        out_shape=(
            jax.ShapeDtypeStruct((local_rows, QW), bf16),
            jax.ShapeDtypeStruct((share, columns), f32),
        ),
        in_specs=[in_vmem, in_vmem, pl.BlockSpec(memory_space=pl.ANY)],
        out_specs=(in_vmem, in_vmem),
        scratch_shapes=[
            pltpu.VMEM((parts, total, features // parts), bf16),
            pltpu.VMEM((total, QW), bf16),
            pltpu.VMEM((features, columns), bf16),
            pltpu.VMEM((total, columns), bf16),
            pltpu.VMEM((local_rows, QW), f32),
            pltpu.VMEM((total, 2 * D), f32),
            pltpu.VMEM((D, total), bf16),
            pltpu.VMEM((total, columns), bf16),
            pltpu.VMEM((total, D), f32),
            pltpu.VMEM((total, D), f32),
            pltpu.VMEM((features, columns), bf16),
            pltpu.VMEM((share, columns), f32),
            pltpu.VMEM((local_rows, QW), f32),
            pltpu.VMEM((total, 2 * D), f32),
            pltpu.VMEM((parts, 8, 128), f32),
            pltpu.SemaphoreType.DMA((parts + 1,)),
            pltpu.SemaphoreType.DMA,
        ]
        + [pltpu.SemaphoreType.DMA((seq_size,))] * 14
        + [pltpu.SemaphoreType.DMA((parts,))] * 2,
        compiler_params=pltpu.CompilerParams(
            collective_id=0, has_side_effects=True, vmem_limit_bytes=VMEM_BUDGET
        ),
        name="resident",
    )(tokens, cotangent, projection)


def fits(local_rows, features, columns, seq_size, head_size):
    total = local_rows * seq_size
    share = features // seq_size
    held = total * (2 * features + 2 * QW + 12 * columns + 24 * D) + 4 * features * columns
    pairs = seq_size >= 8 and seq_size & (seq_size - 1) == 0 and head_size == 4
    aligned = share % 128 == 0 and (features // head_size) % share == 0 and local_rows % 128 == 0
    return pairs and aligned and held < VMEM_BUDGET // 2


def step(tokens, projection, context_cotangent):
    sizes = (*tokens.shape, projection.shape[1], lax.axis_size("seq"), lax.axis_size("head"))
    if fits(*sizes):
        return resident_step(tokens, projection, context_cotangent)
    return on_device(tokens, projection, context_cotangent)


def solution(mesh):
    return jax.shard_map(
        step,
        mesh=mesh,
        in_specs=(P("seq", None), P(None, "head"), P("seq", "head")),
        out_specs=(P("seq", "head"), P("seq", "head")),
        check_vma=False,
    )
```
